512 devices in a mesh: dp: 16 (over z_hi, x), shard: 32 (over y, z_lo, core).
Axes of the slice: x: 4, y: 4, z: 16 (z_hi: 4, z_lo: 4; z = z_hi * 4 + z_lo), core: 2. Of those that a mesh axis runs over, the one named last changes fastest.
Arguments:
- inputs: bfloat16 [2, 4096, 8192], P(None, 'dp', 'shard'), may hold values from -6 to 6
- key_panel: bfloat16 [8192, 4096], P('dp', 'shard'), may hold values from -0.0625 to 0.0625
- value_panel: bfloat16 [8192, 4096], P('dp', 'shard'), may hold values from -0.0625 to 0.0625
- short_filters: float32 [2, 4096, 7], P(None, 'shard'), may hold values from -2 to 2
- medium_filters: float32 [256, 128], P('shard'), may hold values from -0.5 to 0.5
- lengths: int32 [2], replicated, may hold values from 2048 to 4096, as said below
- cotangent: bfloat16 [2, 4096, 4096], P(None, 'dp', 'shard'), may hold values from -0.099609375 to 0.099609375
Outputs:
- mixed: bfloat16 [2, 4096, 4096], P(None, 'dp', 'shard')
- key_grad: bfloat16 [8192, 4096], P('dp', 'shard')
- value_grad: bfloat16 [8192, 4096], P('dp', 'shard')
- short_grad: float32 [2, 4096, 7], P(None, 'shard')
- medium_grad: float32 [256, 128], P('shard')
The draws below stay inside these ranges and needn't reach their ends.
Inputs may be any that keep to these rules, and one draw needn't show every extreme that they name: `lengths`: each length is a multiple of 16; one window in every draw has the full length 4096, the others are shorter.
All inputs are finite; a program needn't handle non-finite values.
Results may differ from the reference program's by a relative error of at most 0.014.
Values may be sent and summed in bfloat16 or wider, within the bound.
No kernel may reach another device: no remote copies, remote signals or barrier semaphores. Data moves between devices by JAX's collectives and lax.ppermute only.
A program may use at most 64 MiB of HBM per device.

```python
import jax
import jax.numpy as jnp
from jax import lax

D = 8192
SHORT = 7
MEDIUM = 128
GROUP = 16
C = 4096
SEQS = 2
LEN_DEV = 256
LEN = 4096
GROUPS = 256
N_DP = 16


def draw_lengths(key, part):
    first_key, second_key = jax.random.split(key)
    steps_all = LEN // 16
    drawn = jax.random.randint(first_key, (SEQS,), steps_all // 2, steps_all) * 16
    longest = jax.random.randint(second_key, (), 0, SEQS)
    chosen = jnp.arange(SEQS) == longest
    return jnp.where(chosen, LEN, drawn).astype(jnp.int32)


def levels(rng, extent, cuts, low, top_value):
    def one(position, parts):
        heights = jax.random.uniform(jax.random.fold_in(jax.random.fold_in(rng, 6), position), (parts,), jnp.float32, low / len(cuts), top_value / len(cuts))
        return jnp.repeat(jnp.exp(heights), extent[position] // parts).reshape((-1,) + (1,) * (len(extent) - position - 1))

    factor_of = one(*cuts[0])
    for cut in cuts[1:]:
        factor_of = factor_of * one(*cut)
    return factor_of


def noise(stream_key, extent, spread, reach, cuts=(), kind=jnp.bfloat16):
    values = jax.random.normal(stream_key, extent, jnp.float32) * spread
    if len(cuts) > 0:
        values = levels(stream_key, extent, cuts, -0.22, 0.18) * values
    return jnp.clip(values, min=-reach, max=reach).astype(kind)


def setup_inputs(seed: int = 0) -> dict:
    seeds = jax.random.split(jax.random.key(seed), 8)
    return {
        "inputs": noise(seeds[0], (SEQS, LEN, D), 1.0, 6.0, ((1, 16), (2, 32))),
        "key_panel": noise(seeds[1], (D, C), D ** -0.5, 0.0625, ((0, 16), (1, 32))),
        "value_panel": noise(seeds[2], (D, C), D ** -0.5, 0.0625, ((0, 16), (1, 32))),
        "short_filters": noise(seeds[3], (2, C, SHORT), 0.38, 2.0, ((1, 32),), jnp.float32),
        "medium_filters": noise(seeds[4], (GROUPS, MEDIUM), 0.088, 0.5, ((0, 32),), jnp.float32),
        "lengths": draw_lengths(jax.random.fold_in(seeds[7], 71), 0),
        "cotangent": noise(seeds[6], (SEQS, LEN, C), 0.015625, 0.099609375, ((1, 16), (2, 32))),
    }


def rounded(values):
    return lax.optimization_barrier(values.astype(jnp.bfloat16)).astype(jnp.float32)

def delay(values, steps):
    count = values.shape[1]
    return jnp.pad(values, ((0, 0), (steps, 0), (0, 0)))[:, :count]

def advance(values, steps):
    return jnp.pad(values, ((0, 0), (0, steps), (0, 0)))[:, steps:]

def short_forward(values, filters):
    total = jnp.zeros(values.shape, jnp.float32)
    for tap in range(SHORT):
        total = total + filters[:, tap] * delay(values, tap)
    return total

def short_backward(grads, filters):
    total = jnp.zeros(grads.shape, jnp.float32)
    for tap in range(SHORT):
        total = total + filters[:, tap] * advance(grads, tap)
    return total

def short_filter_grad(grads, values):
    return jnp.stack([lax.optimization_barrier(jnp.sum(grads * delay(values, tap), axis=(0, 1))) for tap in range(SHORT)], axis=-1)

def medium_forward(product, per_channel):
    padded = jnp.pad(product, ((0, 0), (MEDIUM - 1, 0), (0, 0)))

    def step(tap, total):
        column = lax.dynamic_slice_in_dim(per_channel, tap, 1, 1)[:, 0]
        return total + column * lax.dynamic_slice_in_dim(padded, MEDIUM - 1 - tap, LEN, 1)
    return lax.fori_loop(0, MEDIUM, step, jnp.zeros(product.shape, jnp.float32))

def medium_backward(upstream, per_channel):
    padded = jnp.pad(upstream, ((0, 0), (0, MEDIUM - 1), (0, 0)))

    def step(tap, total):
        column = lax.dynamic_slice_in_dim(per_channel, tap, 1, 1)[:, 0]
        return total + column * lax.dynamic_slice_in_dim(padded, tap, LEN, 1)
    return lax.fori_loop(0, MEDIUM, step, jnp.zeros(upstream.shape, jnp.float32))

def medium_filter_grad(upstream, product):
    padded = jnp.pad(product, ((0, 0), (MEDIUM - 1, 0), (0, 0)))

    def step(carry, tap):
        shifted = lax.dynamic_slice_in_dim(padded, MEDIUM - 1 - tap, LEN, 1)
        return (carry, lax.optimization_barrier(jnp.sum(upstream * shifted, axis=(0, 1))))
    _, sums = lax.scan(step, jnp.zeros((), jnp.float32), jnp.arange(MEDIUM))
    return sums.T.reshape(GROUPS, GROUP, MEDIUM).sum(axis=1)

def reference(inputs, key_panel, value_panel, short_filters, medium_filters, lengths, cotangent):
    flat = inputs.reshape(SEQS * LEN, D)
    keys = rounded(jnp.dot(flat, key_panel, preferred_element_type=jnp.float32)).reshape(SEQS, LEN, C)
    values = rounded(jnp.dot(flat, value_panel, preferred_element_type=jnp.float32)).reshape(SEQS, LEN, C)
    smooth_keys = short_forward(keys, short_filters[0])
    smooth_values = short_forward(values, short_filters[1])
    product = rounded(smooth_keys * smooth_values)
    per_channel = jnp.repeat(medium_filters, GROUP, axis=0)
    response = medium_forward(product, per_channel)
    positions = jnp.arange(LEN)
    live = (positions[None, :] < lengths[:, None]).astype(jnp.float32)[:, :, None]
    mixed = (response * live).astype(jnp.bfloat16)
    upstream = cotangent.astype(jnp.float32) * live
    product_grad = medium_backward(upstream, per_channel)
    medium_grad = medium_filter_grad(upstream, product)
    key_smooth_grad = product_grad * smooth_values
    value_smooth_grad = product_grad * smooth_keys
    short_grad = jnp.stack([short_filter_grad(key_smooth_grad, keys), short_filter_grad(value_smooth_grad, values)])
    key_act = short_backward(key_smooth_grad, short_filters[0]).astype(jnp.bfloat16)
    value_act = short_backward(value_smooth_grad, short_filters[1]).astype(jnp.bfloat16)
    both_grads = jnp.concatenate([key_act, value_act], axis=2)

    def accumulate(index, total):
        begin = index * LEN_DEV
        block = lax.dynamic_slice_in_dim(inputs, begin, LEN_DEV, 1).reshape(SEQS * LEN_DEV, D)
        grad_block = lax.dynamic_slice_in_dim(both_grads, begin, LEN_DEV, 1).reshape(SEQS * LEN_DEV, 2 * C)
        partial_sum = lax.dot_general(block, grad_block, (((0,), (0,)), ((), ())), preferred_element_type=jnp.float32)
        return total + rounded(partial_sum)
    summed = lax.fori_loop(0, N_DP, accumulate, jnp.zeros((D, 2 * C), jnp.float32))
    key_grad = summed[:, :C].astype(jnp.bfloat16)
    value_grad = summed[:, C:].astype(jnp.bfloat16)
    return (mixed, key_grad, value_grad, short_grad, medium_grad)
```

```python
import jax
import jax.numpy as jnp
from jax import lax
from jax.experimental import pallas as pl
from jax.experimental.pallas import tpu as pltpu
from jax.sharding import PartitionSpec as P

BF = jnp.bfloat16
F32 = jnp.float32


def dp_move(value, dzh, dx):
    pairs = [
        (zh * 4 + x, ((zh + dzh) % 4) * 4 + (x + dx) % 4) for zh in range(4) for x in range(4)
    ]
    return lax.ppermute(value, "dp", pairs)


def dp_xor(value, mask):
    return lax.ppermute(value, "dp", [(i, i ^ mask) for i in range(16)])


def y_move(value, dy):
    return lax.ppermute(value, "shard", [(i, (i + 8 * dy) % 32) for i in range(32)])


def shard_xor(value, mask):
    return lax.ppermute(value, "shard", [(i, i ^ mask) for i in range(32)])


def shifted(value, steps):
    first, last = (max(0, -steps), min(16, 16 - steps))
    return lax.ppermute(value, "dp", [(i, i + steps) for i in range(first, last)])


def gather_inputs(block):
    near = jnp.stack([block] + [shard_xor(block, k << 1) for k in (1, 2, 3)])
    up = y_move(near, 1)
    down = y_move(near, -1)
    far_up = y_move(up[:2], 1)
    far_down = y_move(down[2:], -1)
    mine = (near, up, down, far_up, far_down)
    return mine, tuple(shard_xor(piece, 1) for piece in mine)


def gather_panels(block):
    half = block.shape[0] // 2
    up = dp_move(block, 1, 0)
    down = dp_move(block, -1, 0)
    far = jnp.concatenate([dp_move(up[:half], 1, 0), dp_move(down[half:], -1, 0)])
    near = jnp.stack([block, up, down, far])
    east = dp_move(near, 0, 1)
    west = dp_move(near, 0, -1)
    return near, east, west, dp_move(east[:2], 0, 1), dp_move(west[2:], 0, -1)


X_REL = ((0, 0), (3, 0), (1, 0), (2, 0), (2, 2))
W_SLOT = ((0, 0), (3, 0), (1, 0), (2, 0), (2, 2))
ZH_REL = (0, 3, 1, 2)


def fetch_x(idx_ref, x_refs, x_buf, x_sem):
    for core_rel in range(2):
        for piece, ref in enumerate(x_refs[core_rel * 5 : core_rel * 5 + 5]):
            rel, first = X_REL[piece]
            for k in range(ref.shape[0]):
                slot = (
                    lax.rem(idx_ref[2] + rel, 4) * 8
                    + (idx_ref[3] ^ (first + k)) * 2
                    + (idx_ref[4] ^ core_rel)
                )
                pltpu.make_async_copy(ref.at[k], x_buf.at[slot], x_sem.at[slot]).start()


def forward_kernel(idx_ref, *refs):
    x_refs, w_refs, (out_ref, x_buf, w_buf, x_sem, w_sem) = refs[:10], refs[10:15], refs[15:]
    for piece, ref in enumerate(w_refs):
        rel, first = W_SLOT[piece]
        for k in range(ref.shape[0]):
            slot = lax.rem(idx_ref[0] + ZH_REL[first + k], 4) * 4 + lax.rem(idx_ref[1] + rel, 4)
            pltpu.make_async_copy(ref.at[k], w_buf.at[slot], w_sem.at[slot]).start()
    fetch_x(idx_ref, x_refs, x_buf, x_sem)
    depth = x_buf.shape[2]
    total = jnp.zeros(out_ref.shape, F32)
    for slot in range(16):
        pltpu.make_async_copy(w_refs[0].at[0], w_buf.at[slot], w_sem.at[slot]).wait()
        for core in range(2):
            block = slot * 2 + core
            pltpu.make_async_copy(x_refs[0].at[0], x_buf.at[block], x_sem.at[block]).wait()
            total = total + jnp.dot(
                x_buf[block],
                w_buf[slot, core * depth : (core + 1) * depth],
                preferred_element_type=F32,
            )
    out_ref[...] = total.astype(BF)


def forward_matmul(idx, mine, other, panels):
    rows, depth = mine[0].shape[1:]
    width = panels[0].shape[2]
    return pl.pallas_call(
        forward_kernel,
        out_shape=jax.ShapeDtypeStruct((rows, width), BF),
        in_specs=[pl.BlockSpec(memory_space=pltpu.SMEM)]
        + [pl.BlockSpec(memory_space=pl.ANY)] * 15,
        out_specs=pl.BlockSpec(memory_space=pltpu.VMEM),
        scratch_shapes=[
            pltpu.VMEM((32, rows, depth), BF),
            pltpu.VMEM((16, 2 * depth, width), BF),
            pltpu.SemaphoreType.DMA((32,)),
            pltpu.SemaphoreType.DMA((16,)),
        ],
        compiler_params=pltpu.CompilerParams(vmem_limit_bytes=40 << 20),
    )(idx, *mine, *other, *panels)


X_DEST = (2, 1, 3, 0)


def backward_kernel(idx_ref, *refs):
    x_refs, grad_ref, outs, (x_buf, x_sem) = refs[:10], refs[10], refs[11:15], refs[15:]
    fetch_x(idx_ref, x_refs, x_buf, x_sem)
    for block in range(32):
        pltpu.make_async_copy(x_refs[0].at[0], x_buf.at[block], x_sem.at[block]).wait()
    depth = x_buf.shape[2]
    grad = grad_ref[...]
    for out, rel_x in zip(outs, X_DEST):
        for k, rel_zh in enumerate(ZH_REL):
            slot = lax.rem(idx_ref[0] + rel_zh, 4) * 8 + lax.rem(idx_ref[1] + rel_x, 4) * 2
            for core in range(2):
                out[k, :, core * depth : (core + 1) * depth] = jnp.dot(
                    grad, x_buf[slot + core], preferred_element_type=F32
                ).astype(BF)


def backward_matmul(idx, mine, other, grad):
    rows, depth = mine[0].shape[1:]
    width = grad.shape[0]
    return pl.pallas_call(
        backward_kernel,
        out_shape=[jax.ShapeDtypeStruct((4, width, 2 * depth), BF)] * 4,
        in_specs=[pl.BlockSpec(memory_space=pltpu.SMEM)]
        + [pl.BlockSpec(memory_space=pl.ANY)] * 10
        + [pl.BlockSpec(memory_space=pltpu.VMEM)],
        out_specs=[pl.BlockSpec(memory_space=pltpu.VMEM)] * 4,
        scratch_shapes=[
            pltpu.VMEM((32, rows, depth), BF),
            pltpu.SemaphoreType.DMA((32,)),
        ],
        compiler_params=pltpu.CompilerParams(vmem_limit_bytes=40 << 20),
    )(idx, *mine, *other, grad)


def add(*terms):
    total = terms[0].astype(F32)
    for term in terms[1:]:
        total = total + term.astype(F32)
    return total


def ring_reduce(far, plus, minus, own, half, move):
    first = move(far[:half], 1)
    second = move(far[half:], -1)
    early_plus = move(plus[half:], 1)
    early_minus = move(minus[:half], -1)
    late_plus = move(add(plus[:half], first).astype(BF), 1)
    late_minus = move(add(minus[half:], second).astype(BF), -1)
    return jnp.concatenate(
        [add(own[:half], late_plus, early_minus), add(own[half:], early_plus, late_minus)]
    )


def scatter_grads(far, plus, minus, own):
    summed = ring_reduce(far, plus, minus, own, 2, lambda v, s: dp_move(v, 0, s))
    sent = summed.astype(BF)
    return ring_reduce(
        sent[3],
        sent[2],
        sent[1],
        summed[0],
        summed.shape[1] // 2,
        lambda v, s: dp_move(v, s, 0),
    )


def sum_dp(value):
    for mask in (1, 2, 4, 8):
        value = value + dp_xor(value, mask)
    return value


def band(filters, count):
    groups, taps = filters.shape
    width = count + taps - 1
    padded = jnp.concatenate([filters, jnp.zeros((groups, count), filters.dtype)], axis=1)
    tiled = jnp.tile(padded, (1, count))[:, : count * width]
    return tiled.reshape(groups, count, width)


def band_sums(correlation, count, taps):
    groups, _, width = correlation.shape
    flat = correlation.reshape(groups, count * width)
    padded = jnp.concatenate([flat, jnp.zeros((groups, count), F32)], axis=1)
    skewed = padded.reshape(groups, count, width + 1)
    return jnp.sum(skewed, axis=1)[:, :taps][:, ::-1]


def short_taps(extended, filters, count):
    width = filters.shape[-1]
    total = jnp.zeros(extended.shape[:2] + (count, extended.shape[3]), F32)
    for tap in range(width):
        begin = width - 1 - tap
        total = total + filters[:, None, None, :, tap] * extended[
            :, :, begin : begin + count
        ].astype(F32)
    return total


def short_ahead(extended, filters, count):
    width = filters.shape[-1]
    total = jnp.zeros(extended.shape[:2] + (count, extended.shape[3]), F32)
    for tap in range(width):
        total = total + filters[:, None, None, :, tap] * extended[:, :, tap : tap + count]
    return total


def filter_terms(grads, extended, count, width):
    columns = []
    for tap in range(width):
        begin = width - 1 - tap
        columns.append(
            jnp.sum(grads * extended[:, :, begin : begin + count].astype(F32), axis=(1, 2))
        )
    return jnp.stack(columns, axis=-1)


def shards(inputs, key_panel, value_panel, short_filters, medium_filters, lengths, cotangent):
    seqs, count, local_width = inputs.shape
    channels = key_panel.shape[1]
    groups, taps = medium_filters.shape
    group_size = channels // groups
    short_width = short_filters.shape[-1]
    span = count + taps - 1
    dp, shard = lax.axis_index("dp"), lax.axis_index("shard")
    idx = jnp.stack([dp // 4, dp % 4, shard // 8, (shard // 2) % 4, shard % 2]).astype(jnp.int32)

    mine, other = gather_inputs(inputs.reshape(seqs * count, local_width))
    panels = gather_panels(jnp.concatenate([key_panel, value_panel], axis=1))

    position = dp * count + jnp.arange(count, dtype=jnp.int32)
    live = (position[None, :] < lengths[:, None])[:, :, None]
    upstream = jnp.where(live, cotangent, jnp.zeros_like(cotangent))
    after = shifted(upstream[:, : taps - 1], -1)
    upstream_ext = jnp.concatenate([upstream, after], axis=1).reshape(
        seqs, span, groups, group_size
    )
    short_medium = medium_filters.astype(BF)
    product_grad = jnp.einsum(
        "gtr,srgm->stgm", band(short_medium, count), upstream_ext, preferred_element_type=F32
    ).reshape(seqs, count, channels)
    forward_band = band(short_medium[:, ::-1], count)

    projected = forward_matmul(idx, mine, other, panels)
    paired = projected.reshape(seqs, count, 2, channels).transpose(2, 0, 1, 3)
    head_rows = shifted(paired[:, :, count - (short_width - 1) :], 1)
    extended = jnp.concatenate([head_rows, paired], axis=2)
    smoothed = short_taps(extended, short_filters, count)
    product = (smoothed[0] * smoothed[1]).astype(BF)
    before = shifted(product[:, count - (taps - 1) :], 1)
    product_ext = jnp.concatenate([before, product], axis=1).reshape(seqs, span, groups, group_size)
    response = jnp.einsum(
        "gtr,srgm->stgm", forward_band, product_ext, preferred_element_type=F32
    ).reshape(seqs, count, channels)
    mixed = jnp.where(live, response, 0.0).astype(BF)
    correlation = jnp.einsum(
        "stgm,srgm->gtr",
        upstream.reshape(seqs, count, groups, group_size),
        product_ext,
        preferred_element_type=F32,
    )
    medium_local = band_sums(correlation, count, taps)
    smooth_grad = jnp.stack([product_grad * smoothed[1], product_grad * smoothed[0]])
    short_local = filter_terms(smooth_grad, extended, count, short_width)
    ahead_rows = shifted(smooth_grad[:, :, : short_width - 1], -1)
    pair_grad = short_ahead(
        jnp.concatenate([smooth_grad, ahead_rows], axis=2), short_filters, count
    )
    outgoing = pair_grad.astype(BF).transpose(0, 3, 1, 2).reshape(2 * channels, seqs * count)
    grads = scatter_grads(*backward_matmul(idx, mine, other, outgoing)).astype(BF)
    small = sum_dp(
        jnp.concatenate([short_local.reshape(-1), medium_local.reshape(-1)]).reshape(-1, 128)
    ).reshape(-1)
    cut = short_local.size
    return (
        mixed,
        grads[:channels].T,
        grads[channels:].T,
        small[:cut].reshape(short_local.shape),
        small[cut:].reshape(medium_local.shape),
    )


def solution(mesh):
    return jax.shard_map(
        shards,
        mesh=mesh,
        in_specs=(
            P(None, "dp", "shard"),
            P("dp", "shard"),
            P("dp", "shard"),
            P(None, "shard", None),
            P("shard", None),
            P(),
            P(None, "dp", "shard"),
        ),
        out_specs=(
            P(None, "dp", "shard"),
            P("dp", "shard"),
            P("dp", "shard"),
            P(None, "shard", None),
            P("shard", None),
        ),
        check_vma=False,
    )
```

```python
import jax
import jax.numpy as jnp
from jax import lax
from jax.experimental import pallas as pl
from jax.experimental.pallas import tpu as pltpu
from jax.sharding import PartitionSpec as P

BF = jnp.bfloat16
F32 = jnp.float32


def dp_move(value, dzh, dx):
    pairs = [
        (zh * 4 + x, ((zh + dzh) % 4) * 4 + (x + dx) % 4) for zh in range(4) for x in range(4)
    ]
    return lax.ppermute(value, "dp", pairs)


def dp_xor(value, mask):
    return lax.ppermute(value, "dp", [(i, i ^ mask) for i in range(16)])


def shifted(value, steps):
    first, last = (max(0, -steps), min(16, 16 - steps))
    return lax.ppermute(value, "dp", [(i, i + steps) for i in range(first, last)])


def gather_panels(block):
    half = block.shape[0] // 2
    up = dp_move(block, 1, 0)
    down = dp_move(block, -1, 0)
    far_up = dp_move(up[:half], 1, 0)
    far_down = dp_move(down[half:], -1, 0)
    near = jnp.stack([block, up, down])
    east = dp_move(near, 0, 1)
    west = dp_move(near, 0, -1)
    far = jnp.concatenate([far_up, far_down])[None]
    east_far = dp_move(far, 0, 1)
    west_far = dp_move(far, 0, -1)
    two_east = dp_move(east[:2], 0, 1)
    two_west = dp_move(jnp.concatenate([west[2:], west_far]), 0, -1)
    return near, far, east, east_far, west, west_far, two_east, two_west


W_PIECES = ((0, 0), (0, 3), (3, 0), (3, 3), (1, 0), (1, 3), (2, 0), (2, 2))
ZH_REL = (0, 3, 1, 2)


def forward_kernel(idx_ref, x_ref, *refs):
    w_refs, (out_ref, head_ref, x_buf, w_buf, x_sem, w_sem) = refs[:8], refs[8:]
    blocks = x_buf.shape[0]
    for piece, ref in enumerate(w_refs):
        rel, first = W_PIECES[piece]
        for k in range(ref.shape[0]):
            slot = lax.rem(idx_ref[0] + ZH_REL[first + k], 4) * 4 + lax.rem(idx_ref[1] + rel, 4)
            pltpu.make_async_copy(ref.at[k], w_buf.at[slot], w_sem.at[slot]).start()
    for block in range(blocks):
        pltpu.make_async_copy(x_ref.at[block], x_buf.at[block], x_sem.at[block]).start()
    depth = x_buf.shape[2]
    total = jnp.zeros((x_buf.shape[1], w_buf.shape[2]), F32)
    for block in range(blocks):
        slot, core = block // 2, block % 2
        if core == 0:
            pltpu.make_async_copy(w_refs[0].at[0], w_buf.at[slot], w_sem.at[slot]).wait()
        pltpu.make_async_copy(x_ref.at[block], x_buf.at[block], x_sem.at[block]).wait()
        total = total + jnp.dot(
            x_buf[block],
            w_buf[slot, core * depth : (core + 1) * depth],
            preferred_element_type=F32,
        )
    turned = total.T.astype(BF)
    out_ref[...] = turned
    half = turned.shape[1] // 2
    head_ref[:, :128] = turned[:, :128]
    head_ref[:, 128:] = turned[:, half : half + 128]


def forward_matmul(idx, features, panels):
    blocks, rows, depth = features.shape
    width = panels[0].shape[2]
    return pl.pallas_call(
        forward_kernel,
        out_shape=[
            jax.ShapeDtypeStruct((width, rows), BF),
            jax.ShapeDtypeStruct((width, 256), BF),
        ],
        in_specs=[pl.BlockSpec(memory_space=pltpu.SMEM)] + [pl.BlockSpec(memory_space=pl.ANY)] * 9,
        out_specs=[pl.BlockSpec(memory_space=pltpu.VMEM)] * 2,
        scratch_shapes=[
            pltpu.VMEM((blocks, rows, depth), BF),
            pltpu.VMEM((blocks // 2, 2 * depth, width), BF),
            pltpu.SemaphoreType.DMA((blocks,)),
            pltpu.SemaphoreType.DMA((blocks // 2,)),
        ],
        compiler_params=pltpu.CompilerParams(vmem_limit_bytes=40 << 20),
    )(idx, features, *panels)


X_DEST = (2, 1, 3, 0)


def backward_kernel(idx_ref, x_ref, grad_ref, *refs):
    outs, (x_buf, x_sem) = refs[:4], refs[4:]
    depth = x_buf.shape[2]
    order = [(out, k, rel_x, rel) for out, rel_x in zip(outs, X_DEST) for k, rel in enumerate(ZH_REL)]
    copies = []
    for place, (_, _, rel_x, rel) in enumerate(order):
        slot = lax.rem(idx_ref[0] + rel, 4) * 8 + lax.rem(idx_ref[1] + rel_x, 4) * 2
        copy = pltpu.make_async_copy(
            x_ref.at[pl.ds(slot, 2)], x_buf.at[pl.ds(2 * place, 2)], x_sem.at[place]
        )
        copy.start()
        copies.append(copy)
    grad = grad_ref[...]
    for place, (out, k, _, _) in enumerate(order):
        copies[place].wait()
        for core in range(2):
            out[k, :, core * depth : (core + 1) * depth] = jnp.dot(
                grad, x_buf[2 * place + core], preferred_element_type=F32
            ).astype(BF)


def backward_matmul(idx, features, grad):
    blocks, rows, depth = features.shape
    width = grad.shape[0]
    return pl.pallas_call(
        backward_kernel,
        out_shape=[jax.ShapeDtypeStruct((4, width, 2 * depth), BF)] * 4,
        in_specs=[
            pl.BlockSpec(memory_space=pltpu.SMEM),
            pl.BlockSpec(memory_space=pl.ANY),
            pl.BlockSpec(memory_space=pltpu.VMEM),
        ],
        out_specs=[pl.BlockSpec(memory_space=pltpu.VMEM)] * 4,
        scratch_shapes=[
            pltpu.VMEM((blocks, rows, depth), BF),
            pltpu.SemaphoreType.DMA((blocks // 2,)),
        ],
        compiler_params=pltpu.CompilerParams(vmem_limit_bytes=40 << 20),
    )(idx, features, grad)


def toeplitz(row):
    spread = jnp.broadcast_to(row, (256, 256))
    return pltpu.roll(spread, 0, 1, stride=1, stride_axis=0)[:, :128].astype(BF)


def cotangent_kernel(meta_ref, own_ref, next_ref, ahead_ref, behind_ref, up_ref, grad_ref, band_ref, ext):
    for s in range(2):
        base = meta_ref[0]
        place = lax.broadcasted_iota(jnp.int32, (128, 256), 1) + base
        own = own_ref[s].astype(F32).T
        own = jnp.where(place < meta_ref[1 + s], own, 0.0).astype(BF)
        up_ref[:, s * 256 : (s + 1) * 256] = own
        tail = jnp.concatenate([next_ref[s].astype(F32), jnp.zeros((112, 128), F32)]).T
        tail = jnp.where(place + 256 < meta_ref[1 + s], tail, 0.0).astype(BF)
        ext[:, s * 512 : s * 512 + 256] = own
        ext[:, s * 512 + 256 : (s + 1) * 512] = tail
    for g in range(8):
        band_ref[g] = toeplitz(behind_ref[g : g + 1])
        rows = slice(16 * g, 16 * g + 16)
        left = jnp.concatenate(
            [
                ext[rows, s * 512 + 128 * b : s * 512 + 128 * b + 256]
                for s in range(2)
                for b in range(3)
            ]
        )
        total = jnp.dot(left, toeplitz(ahead_ref[g : g + 1]), preferred_element_type=F32)
        for part in range(6):
            grad_ref[rows, part * 128 : part * 128 + 128] = total[part * 16 : part * 16 + 16]


def cotangent_terms(meta, own, after, medium):
    zeros = jnp.zeros((8, 128), F32)
    ahead = jnp.concatenate([medium[:, :1], zeros, medium[:, :0:-1]], axis=1)
    behind = jnp.concatenate([zeros, medium], axis=1)
    return pl.pallas_call(
        cotangent_kernel,
        out_shape=[
            jax.ShapeDtypeStruct((128, 512), BF),
            jax.ShapeDtypeStruct((128, 768), F32),
            jax.ShapeDtypeStruct((8, 256, 128), BF),
        ],
        in_specs=[pl.BlockSpec(memory_space=pltpu.SMEM)] + [pl.BlockSpec(memory_space=pltpu.VMEM)] * 4,
        out_specs=[pl.BlockSpec(memory_space=pltpu.VMEM)] * 3,
        scratch_shapes=[pltpu.VMEM((128, 1024), BF)],
    )(meta, own, after, ahead, behind)


def middle_kernel(
    meta_ref, kv_ref, prev_ref, head_ref, up_ref, grad_ref, band_ref, taps_ref,
    mixed_ref, dy_ref, small_ref, prod, resp,
):
    lanes = lax.broadcasted_iota(jnp.int32, (128, 128), 1)
    sums = jnp.zeros((128, 128), F32)
    partial = [[None] * 7 for _ in range(2)]
    for s in range(2):
        smooth = []
        for b in range(2):
            rows = slice(128 * b, 128 * b + 128)
            ext = jnp.concatenate(
                [
                    prev_ref[rows, s * 256 : (s + 1) * 256],
                    kv_ref[rows, s * 256 : (s + 1) * 256],
                    head_ref[rows, s * 128 : (s + 1) * 128],
                ],
                axis=1,
            ).astype(F32)
            total = taps_ref[rows, 0:1] * ext
            for j in range(1, 7):
                total = total + taps_ref[rows, j : j + 1] * pltpu.roll(ext, j, 1)
            smooth.append(total[:, 128:])
        prod[:, s * 384 : (s + 1) * 384] = (smooth[0][:, :384] * smooth[1][:, :384]).astype(BF)
        for b in range(2):
            rows = slice(128 * b, 128 * b + 128)
            slope = grad_ref[:, s * 384 : (s + 1) * 384] * smooth[1 - b][:, 128:512]
            own = kv_ref[rows, s * 256 : (s + 1) * 256].astype(F32)
            act = jnp.zeros((128, 256), F32)
            for j in range(7):
                moved = (slope if j == 0 else pltpu.roll(slope, 384 - j, 1))[:, :256]
                act = act + taps_ref[rows, j : j + 1] * moved
                both = moved * own
                both = both[:, :128] + both[:, 128:]
                partial[b][j] = both if s == 0 else partial[b][j] + both
            dy_ref[rows, s * 256 : (s + 1) * 256] = act.astype(BF)
    for b in range(2):
        for j in range(7):
            column = jnp.sum(partial[b][j], axis=1, keepdims=True)
            sums = jnp.where(lanes == b * 8 + j, column, sums)
    small_ref[0:16] = sums.T[0:16]
    for g in range(8):
        rows = slice(16 * g, 16 * g + 16)
        left = jnp.concatenate(
            [
                prod[rows, s * 384 + 128 * b : s * 384 + 128 * b + 256]
                for s in range(2)
                for b in range(2)
            ]
        )
        total = jnp.dot(left, band_ref[g], preferred_element_type=F32)
        for part in range(4):
            resp[rows, part * 128 : part * 128 + 128] = total[part * 16 : part * 16 + 16]
        above = jnp.concatenate(
            [up_ref[rows, part * 128 : part * 128 + 128] for part in range(4)]
        )
        folded = lax.dot_general(
            above, left, (((0,), (0,)), ((), ())), preferred_element_type=F32
        )
        count = 64
        while count >= 1:
            folded = folded[:count] + pltpu.roll(folded[count : 2 * count], 256 - count, 1)
            count //= 2
        small_ref[16 + g : 17 + g] = folded[:, :128]
        small_ref[24 + g : 25 + g] = folded[:, 128:]
    for s in range(2):
        place = lax.broadcasted_iota(jnp.int32, (256, 128), 0) + meta_ref[0]
        turned = resp[:, s * 256 : (s + 1) * 256].T
        mixed_ref[s] = jnp.where(place < meta_ref[1 + s], turned, 0.0).astype(BF)


def middle_terms(meta, kv, prev, head, up, grad, bands, short_filters):
    taps = jnp.pad(short_filters.reshape(256, 7), ((0, 0), (0, 1)))
    return pl.pallas_call(
        middle_kernel,
        out_shape=[
            jax.ShapeDtypeStruct((2, 256, 128), BF),
            jax.ShapeDtypeStruct((256, 512), BF),
            jax.ShapeDtypeStruct((32, 128), F32),
        ],
        in_specs=[pl.BlockSpec(memory_space=pltpu.SMEM)] + [pl.BlockSpec(memory_space=pltpu.VMEM)] * 7,
        out_specs=[pl.BlockSpec(memory_space=pltpu.VMEM)] * 3,
        scratch_shapes=[pltpu.VMEM((128, 768), BF), pltpu.VMEM((128, 512), F32)],
    )(meta, kv, prev, head, up, grad, bands, taps)


def add(*terms):
    total = terms[0].astype(F32)
    for term in terms[1:]:
        total = total + term.astype(F32)
    return total


def ring_reduce(far, plus, minus, own, half, move):
    first = move(far[:half], 1)
    second = move(far[half:], -1)
    early_plus = move(plus[half:], 1)
    early_minus = move(minus[:half], -1)
    late_plus = move(add(plus[:half], first).astype(BF), 1)
    late_minus = move(add(minus[half:], second).astype(BF), -1)
    return jnp.concatenate(
        [add(own[:half], late_plus, early_minus), add(own[half:], early_plus, late_minus)]
    )


def scatter_grads(far, plus, minus, own):
    summed = ring_reduce(far, plus, minus, own, 2, lambda v, s: dp_move(v, 0, s))
    sent = summed.astype(BF)
    return ring_reduce(
        sent[3],
        sent[2],
        sent[1],
        summed[0],
        summed.shape[1] // 2,
        lambda v, s: dp_move(v, s, 0),
    )


def sum_dp(value):
    for mask in (1, 2, 4, 8):
        value = value + dp_xor(value, mask)
    return value


def shards(inputs, key_panel, value_panel, short_filters, medium_filters, lengths, cotangent):
    seqs, count, local_width = inputs.shape
    channels = key_panel.shape[1]
    dp = lax.axis_index("dp")
    idx = jnp.stack([dp // 4, dp % 4]).astype(jnp.int32)
    meta = jnp.concatenate([(dp * count).reshape(1).astype(jnp.int32), lengths])

    features = lax.all_gather(inputs.reshape(seqs * count, local_width), "shard", axis=0)
    panels = gather_panels(jnp.concatenate([key_panel, value_panel], axis=1))
    after = shifted(cotangent[:, :144], -1)
    up, product_grad, bands = cotangent_terms(meta, cotangent, after, medium_filters)

    kv, head = forward_matmul(idx, features, panels)
    prev = shifted(kv, 1)
    head = shifted(head, -1)
    mixed, outgoing, small = middle_terms(
        meta, kv, prev, head, up, product_grad, bands, short_filters
    )
    grads = scatter_grads(*backward_matmul(idx, features, outgoing)).astype(BF)
    small = sum_dp(small)
    short_grad = small[:16].reshape(2, 8, channels)[:, :7].transpose(0, 2, 1)
    medium_grad = jnp.concatenate([small[24:, :1], small[16:24, :0:-1]], axis=1)
    return (mixed, grads[:channels].T, grads[channels:].T, short_grad, medium_grad)


def solution(mesh):
    return jax.shard_map(
        shards,
        mesh=mesh,
        in_specs=(
            P(None, "dp", "shard"),
            P("dp", "shard"),
            P("dp", "shard"),
            P(None, "shard", None),
            P("shard", None),
            P(),
            P(None, "dp", "shard"),
        ),
        out_specs=(
            P(None, "dp", "shard"),
            P("dp", "shard"),
            P("dp", "shard"),
            P(None, "shard", None),
            P("shard", None),
        ),
        check_vma=False,
    )
```

```python
import functools

import jax
import jax.numpy as jnp
from jax import lax
from jax.experimental import pallas as pl
from jax.experimental.pallas import tpu as pltpu
from jax.sharding import PartitionSpec as P


BF = jnp.bfloat16
F32 = jnp.float32


def dp_move(value, dzh, dx):
    pairs = [
        (zh * 4 + x, ((zh + dzh) % 4) * 4 + (x + dx) % 4) for zh in range(4) for x in range(4)
    ]
    return lax.ppermute(value, "dp", pairs)


def dp_xor(value, mask):
    return lax.ppermute(value, "dp", [(i, i ^ mask) for i in range(16)])


def shard_xor(value, mask):
    return lax.ppermute(value, "shard", [(i, i ^ mask) for i in range(32)])


def shifted(value, steps):
    first, last = (max(0, -steps), min(16, 16 - steps))
    return lax.ppermute(value, "dp", [(i, i + steps) for i in range(first, last)])


def gather_panels(block):
    half = block.shape[0] // 2
    up = dp_move(block, 1, 0)
    down = dp_move(block, -1, 0)
    far_up = dp_move(up[:half], 1, 0)
    far_down = dp_move(down[half:], -1, 0)
    near = jnp.stack([block, up, down])
    far = jnp.concatenate([far_up, far_down])[None]
    east = dp_move(near, 0, 1)
    west = dp_move(near, 0, -1)
    east_far = dp_move(far, 0, 1)
    west_far = dp_move(far, 0, -1)
    two_east = dp_move(east[:2], 0, 1)
    two_west = dp_move(jnp.concatenate([west[2:], west_far]), 0, -1)
    return near, far, east, east_far, west, west_far, two_east, two_west


W_PIECES = ((0, 0), (0, 3), (3, 0), (3, 3), (1, 0), (1, 3), (2, 0), (2, 2))
ZH_REL = (0, 3, 1, 2)


def forward_kernel(idx_ref, mine_ref, other_ref, *refs):
    w_refs, (out_ref, head_ref, x_buf, w_buf, x_sem, w_sem) = refs[:8], refs[8:]
    slots = x_buf.shape[0]
    for slot in range(slots):
        for flip, ref in enumerate((mine_ref, other_ref)):
            core = idx_ref[2] ^ flip
            pltpu.make_async_copy(ref.at[slot], x_buf.at[slot, core], x_sem.at[slot, core]).start()
    for piece, ref in enumerate(w_refs):
        rel, first = W_PIECES[piece]
        for k in range(ref.shape[0]):
            slot = lax.rem(idx_ref[0] + ZH_REL[first + k], 4) * 4 + lax.rem(idx_ref[1] + rel, 4)
            pltpu.make_async_copy(ref.at[k], w_buf.at[slot], w_sem.at[slot]).start()
    depth = x_buf.shape[3]
    total = jnp.zeros((x_buf.shape[2], w_buf.shape[2]), F32)
    for slot in range(slots):
        pltpu.make_async_copy(w_refs[0].at[0], w_buf.at[slot], w_sem.at[slot]).wait()
        for core in range(2):
            pltpu.make_async_copy(mine_ref.at[0], x_buf.at[slot, core], x_sem.at[slot, core]).wait()
            total = total + jnp.dot(
                x_buf[slot, core],
                w_buf[slot, core * depth : (core + 1) * depth],
                preferred_element_type=F32,
            )
    turned = total.T.astype(BF)
    out_ref[...] = turned
    half = turned.shape[1] // 2
    head_ref[:, :128] = turned[:, :128]
    head_ref[:, 128:] = turned[:, half : half + 128]


def forward_matmul(idx, mine, other, panels):
    slots, rows, depth = mine.shape
    width = panels[0].shape[2]
    return pl.pallas_call(
        forward_kernel,
        out_shape=[
            jax.ShapeDtypeStruct((width, rows), BF),
            jax.ShapeDtypeStruct((width, 256), BF),
        ],
        in_specs=[pl.BlockSpec(memory_space=pltpu.SMEM)]
        + [pl.BlockSpec(memory_space=pltpu.HBM)] * 2
        + [pl.BlockSpec(memory_space=pl.ANY)] * 8,
        out_specs=[pl.BlockSpec(memory_space=pltpu.VMEM)] * 2,
        scratch_shapes=[
            pltpu.VMEM((slots, 2, rows, depth), BF),
            pltpu.VMEM((slots, 2 * depth, width), BF),
            pltpu.SemaphoreType.DMA((slots, 2)),
            pltpu.SemaphoreType.DMA((slots,)),
        ],
        compiler_params=pltpu.CompilerParams(vmem_limit_bytes=40 << 20),
    )(idx, mine, other, *panels)


def backward_kernel(rels, idx_ref, mine_ref, other_ref, grad_ref, east, west, keep_e, keep_w, own, x_buf, x_sem):
    depth = x_buf.shape[3]
    half = grad_ref.shape[0] // 2
    order = [(rel_x, k, rel) for rel_x in (2, 1, 3, 0) for k, rel in enumerate(rels)]
    for place, (rel_x, _, rel) in enumerate(order):
        slot = lax.rem(idx_ref[0] + rel, 4) * 4 + lax.rem(idx_ref[1] + rel_x, 4)
        for flip, ref in enumerate((mine_ref, other_ref)):
            core = idx_ref[2] ^ flip
            pltpu.make_async_copy(ref.at[slot], x_buf.at[place, core], x_sem.at[place, core]).start()
    grad = grad_ref[...]
    for place, (rel_x, k, _) in enumerate(order):
        for core in range(2):
            columns = slice(core * depth, (core + 1) * depth)
            pltpu.make_async_copy(mine_ref.at[0], x_buf.at[place, core], x_sem.at[place, core]).wait()
            part = jnp.dot(grad, x_buf[place, core], preferred_element_type=F32).astype(BF)
            low, high = part[:half], part[half:]
            if rel_x == 2:
                east[0, k, :, columns] = low
                west[0, k, :, columns] = high
            elif rel_x == 1:
                keep_e[k, :, columns] = low
                east[1, k, :, columns] = high
            elif rel_x == 3:
                west[1, k, :, columns] = low
                keep_w[k, :, columns] = high
            else:
                own[0, k, :, columns] = low
                own[1, k, :, columns] = high


def backward_matmul(rels, idx, mine, other, grad):
    _, rows, depth = mine.shape
    count, half = len(rels), grad.shape[0] // 2
    one = jax.ShapeDtypeStruct((count, half, 2 * depth), BF)
    two = jax.ShapeDtypeStruct((2, count, half, 2 * depth), BF)
    return pl.pallas_call(
        functools.partial(backward_kernel, rels),
        out_shape=[two, two, one, one, two],
        in_specs=[pl.BlockSpec(memory_space=pltpu.SMEM)]
        + [pl.BlockSpec(memory_space=pltpu.HBM)] * 2
        + [pl.BlockSpec(memory_space=pltpu.VMEM)],
        out_specs=[pl.BlockSpec(memory_space=pltpu.VMEM)] * 5,
        scratch_shapes=[
            pltpu.VMEM((4 * count, 2, rows, depth), BF),
            pltpu.SemaphoreType.DMA((4 * count, 2)),
        ],
        compiler_params=pltpu.CompilerParams(vmem_limit_bytes=40 << 20),
    )(idx, mine, other, grad)


def toeplitz(row):
    spread = jnp.broadcast_to(row, (256, 256))
    return pltpu.roll(spread, 0, 1, stride=1, stride_axis=0)[:, :128].astype(BF)


def cotangent_kernel(meta_ref, own_ref, next_ref, ahead_ref, behind_ref, up_ref, grad_ref, band_ref, ext):
    for s in range(2):
        base = meta_ref[0]
        place = lax.broadcasted_iota(jnp.int32, (128, 256), 1) + base
        own = own_ref[s].astype(F32).T
        own = jnp.where(place < meta_ref[1 + s], own, 0.0).astype(BF)
        up_ref[:, s * 256 : (s + 1) * 256] = own
        tail = jnp.concatenate([next_ref[s].astype(F32), jnp.zeros((112, 128), F32)]).T
        tail = jnp.where(place + 256 < meta_ref[1 + s], tail, 0.0).astype(BF)
        ext[:, s * 512 : s * 512 + 256] = own
        ext[:, s * 512 + 256 : (s + 1) * 512] = tail
    for g in range(8):
        band_ref[g] = toeplitz(behind_ref[g : g + 1])
        rows = slice(16 * g, 16 * g + 16)
        left = jnp.concatenate(
            [
                ext[rows, s * 512 + 128 * b : s * 512 + 128 * b + 256]
                for s in range(2)
                for b in range(3)
            ]
        )
        total = jnp.dot(left, toeplitz(ahead_ref[g : g + 1]), preferred_element_type=F32)
        for part in range(6):
            grad_ref[rows, part * 128 : part * 128 + 128] = total[part * 16 : part * 16 + 16]


def cotangent_terms(meta, own, after, medium):
    zeros = jnp.zeros((8, 128), F32)
    ahead = jnp.concatenate([medium[:, :1], zeros, medium[:, :0:-1]], axis=1)
    behind = jnp.concatenate([zeros, medium], axis=1)
    return pl.pallas_call(
        cotangent_kernel,
        out_shape=[
            jax.ShapeDtypeStruct((128, 512), BF),
            jax.ShapeDtypeStruct((128, 768), F32),
            jax.ShapeDtypeStruct((8, 256, 128), BF),
        ],
        in_specs=[pl.BlockSpec(memory_space=pltpu.SMEM)] + [pl.BlockSpec(memory_space=pltpu.VMEM)] * 4,
        out_specs=[pl.BlockSpec(memory_space=pltpu.VMEM)] * 3,
        scratch_shapes=[pltpu.VMEM((128, 1024), BF)],
    )(meta, own, after, ahead, behind)


def middle_kernel(
    kv_ref, prev_ref, head_ref, grad_ref, taps_ref, dy_ref, prod_ref, sums_ref
):
    lanes = lax.broadcasted_iota(jnp.int32, (128, 128), 1)
    sums = jnp.zeros((128, 128), F32)
    partial = [[None] * 7 for _ in range(2)]
    for s in range(2):
        smooth = []
        for b in range(2):
            rows = slice(128 * b, 128 * b + 128)
            ext = jnp.concatenate(
                [
                    prev_ref[rows, s * 256 : (s + 1) * 256],
                    kv_ref[rows, s * 256 : (s + 1) * 256],
                    head_ref[rows, s * 128 : (s + 1) * 128],
                ],
                axis=1,
            ).astype(F32)
            total = taps_ref[rows, 0:1] * ext
            for j in range(1, 7):
                total = total + taps_ref[rows, j : j + 1] * pltpu.roll(ext, j, 1)
            smooth.append(total[:, 128:])
        prod_ref[:, s * 384 : (s + 1) * 384] = (smooth[0][:, :384] * smooth[1][:, :384]).astype(BF)
        for b in range(2):
            rows = slice(128 * b, 128 * b + 128)
            slope = grad_ref[:, s * 384 : (s + 1) * 384] * smooth[1 - b][:, 128:512]
            own = kv_ref[rows, s * 256 : (s + 1) * 256].astype(F32)
            act = jnp.zeros((128, 256), F32)
            for j in range(7):
                moved = (slope if j == 0 else pltpu.roll(slope, 384 - j, 1))[:, :256]
                act = act + taps_ref[rows, j : j + 1] * moved
                both = moved * own
                both = both[:, :128] + both[:, 128:]
                partial[b][j] = both if s == 0 else partial[b][j] + both
            dy_ref[rows, s * 256 : (s + 1) * 256] = act.astype(BF)
    for b in range(2):
        for j in range(7):
            column = jnp.sum(partial[b][j], axis=1, keepdims=True)
            sums = jnp.where(lanes == b * 8 + j, column, sums)
    sums_ref[...] = sums.T[0:16]


def middle_terms(kv, prev, head, grad, short_filters):
    taps = jnp.pad(short_filters.reshape(256, 7), ((0, 0), (0, 1)))
    return pl.pallas_call(
        middle_kernel,
        out_shape=[
            jax.ShapeDtypeStruct((256, 512), BF),
            jax.ShapeDtypeStruct((128, 768), BF),
            jax.ShapeDtypeStruct((16, 128), F32),
        ],
        in_specs=[pl.BlockSpec(memory_space=pltpu.VMEM)] * 5,
        out_specs=[pl.BlockSpec(memory_space=pltpu.VMEM)] * 3,
    )(kv, prev, head, grad, taps)


def response_kernel(meta_ref, prod, up_ref, band_ref, sums_ref, mixed_ref, small_ref, resp):
    small_ref[0:16] = sums_ref[...]
    for g in range(8):
        rows = slice(16 * g, 16 * g + 16)
        left = jnp.concatenate(
            [
                prod[rows, s * 384 + 128 * b : s * 384 + 128 * b + 256]
                for s in range(2)
                for b in range(2)
            ]
        )
        total = jnp.dot(left, band_ref[g], preferred_element_type=F32)
        for part in range(4):
            resp[rows, part * 128 : part * 128 + 128] = total[part * 16 : part * 16 + 16]
        above = jnp.concatenate(
            [up_ref[rows, part * 128 : part * 128 + 128] for part in range(4)]
        )
        folded = lax.dot_general(
            above, left, (((0,), (0,)), ((), ())), preferred_element_type=F32
        )
        count = 64
        while count >= 1:
            folded = folded[:count] + pltpu.roll(folded[count : 2 * count], 256 - count, 1)
            count //= 2
        small_ref[16 + g : 17 + g] = folded[:, :128]
        small_ref[24 + g : 25 + g] = folded[:, 128:]
    for s in range(2):
        place = lax.broadcasted_iota(jnp.int32, (256, 128), 0) + meta_ref[0]
        turned = resp[:, s * 256 : (s + 1) * 256].T
        mixed_ref[s] = jnp.where(place < meta_ref[1 + s], turned, 0.0).astype(BF)


def response_terms(meta, prod, up, bands, sums):
    return pl.pallas_call(
        response_kernel,
        out_shape=[
            jax.ShapeDtypeStruct((2, 256, 128), BF),
            jax.ShapeDtypeStruct((32, 128), F32),
        ],
        in_specs=[pl.BlockSpec(memory_space=pltpu.SMEM)] + [pl.BlockSpec(memory_space=pltpu.VMEM)] * 4,
        out_specs=[pl.BlockSpec(memory_space=pltpu.VMEM)] * 2,
        scratch_shapes=[pltpu.VMEM((128, 512), F32)],
    )(meta, prod, up, bands, sums)


def add(*terms):
    total = terms[0].astype(F32)
    for term in terms[1:]:
        total = total + term.astype(F32)
    return total


def x_ring(parts):
    east, west, keep_e, keep_w, own = parts
    from_west = dp_move(east, 0, 1)
    from_east = dp_move(west, 0, -1)
    low = add(keep_e, from_west[0]).astype(BF)
    high = add(keep_w, from_east[0]).astype(BF)
    low = dp_move(low, 0, 1)
    high = dp_move(high, 0, -1)
    return (own[0], from_east[1], low), (own[1], from_west[1], high)


def sum_dp(value):
    for mask in (1, 2, 4, 8):
        moved = dp_xor(value, mask)
        value = value + moved
    return value


def finish_kernel(*refs):
    for terms, out in ((refs[0:5], refs[10]), (refs[5:10], refs[11])):
        total = terms[0][...].astype(F32)
        for term in terms[1:]:
            total = total + term[...].astype(F32)
        out[...] = total.T.astype(BF)


def finish(low, high):
    half, rows = low[0].shape
    return pl.pallas_call(
        finish_kernel,
        out_shape=[jax.ShapeDtypeStruct((rows, half), BF)] * 2,
        in_specs=[pl.BlockSpec(memory_space=pltpu.VMEM)] * 10,
        out_specs=[pl.BlockSpec(memory_space=pltpu.VMEM)] * 2,
    )(*low, *high)


def body(inputs, key_panel, value_panel, short_filters, medium_filters, lengths, cotangent):
    seqs, count, local_width = inputs.shape
    channels = key_panel.shape[1]
    dp, shard = lax.axis_index("dp"), lax.axis_index("shard")
    idx = jnp.stack([dp // 4, dp % 4, shard % 2]).astype(jnp.int32)
    meta = jnp.concatenate([(dp * count).reshape(1).astype(jnp.int32), lengths])

    same_core = [[2 * i + core for i in range(16)] for core in range(2)]
    mine = lax.all_gather(
        inputs.reshape(seqs * count, local_width), "shard", axis=0, axis_index_groups=same_core
    )
    other = shard_xor(mine, 1)
    mine = pltpu.with_memory_space_constraint(mine, pltpu.HBM)
    other = pltpu.with_memory_space_constraint(other, pltpu.HBM)
    panels = gather_panels(jnp.concatenate([key_panel, value_panel], axis=1))
    after = shifted(cotangent[:, :144], -1)
    up, product_grad, bands = cotangent_terms(meta, cotangent, after, medium_filters)

    kv, head = forward_matmul(idx, mine, other, panels)
    prev = shifted(kv, 1)
    head = shifted(head, -1)
    outgoing, product, sums = middle_terms(kv, prev, head, product_grad, short_filters)

    far = backward_matmul((2,), idx, mine, other, outgoing)
    near = backward_matmul((1, 3), idx, mine, other, outgoing)
    own = backward_matmul((0,), idx, mine, other, outgoing)
    mixed, small = response_terms(meta, product, up, bands, sums)
    small = sum_dp(small)

    far_low, far_high = (add(*terms)[0].astype(BF) for terms in x_ring(far))
    from_south = dp_move(far_low, 1, 0)
    from_north = dp_move(far_high, -1, 0)
    near_low, near_high = (add(*terms) for terms in x_ring(near))
    north = jnp.stack([add(near_low[0], from_south), near_high[0]]).astype(BF)
    south = jnp.stack([near_low[1], add(near_high[1], from_north)]).astype(BF)
    north = dp_move(north, 1, 0)
    south = dp_move(south, -1, 0)
    own_low, own_high = x_ring(own)
    key_grad, value_grad = finish(
        [term[0] for term in own_low] + [north[0], south[0]],
        [term[0] for term in own_high] + [north[1], south[1]],
    )
    short_grad = small[:16].reshape(2, 8, channels)[:, :7].transpose(0, 2, 1)
    medium_grad = jnp.concatenate([small[24:, :1], small[16:24, :0:-1]], axis=1)
    return (mixed, key_grad, value_grad, short_grad, medium_grad)


def solution(mesh):
    return jax.shard_map(
        body,
        mesh=mesh,
        in_specs=(
            P(None, "dp", "shard"),
            P("dp", "shard"),
            P("dp", "shard"),
            P(None, "shard", None),
            P("shard", None),
            P(),
            P(None, "dp", "shard"),
        ),
        out_specs=(
            P(None, "dp", "shard"),
            P("dp", "shard"),
            P("dp", "shard"),
            P(None, "shard", None),
            P("shard", None),
        ),
        check_vma=False,
    )
```

```python
import functools

import jax
import jax.numpy as jnp
from jax import lax
from jax.experimental import pallas as pl
from jax.experimental.pallas import tpu as pltpu
from jax.sharding import PartitionSpec as P


BF = jnp.bfloat16
F32 = jnp.float32


def dp_move(value, dzh, dx):
    pairs = [
        (zh * 4 + x, ((zh + dzh) % 4) * 4 + (x + dx) % 4) for zh in range(4) for x in range(4)
    ]
    return lax.ppermute(value, "dp", pairs)


def shifted(value, steps):
    first, last = (max(0, -steps), min(16, 16 - steps))
    return lax.ppermute(value, "dp", [(i, i + steps) for i in range(first, last)])


def gather_panels(block):
    half = block.shape[0] // 2
    up = dp_move(block, 1, 0)
    down = dp_move(block, -1, 0)
    far_up = dp_move(up[:half], 1, 0)
    far_down = dp_move(down[half:], -1, 0)
    near = jnp.stack([block, up, down])
    far = jnp.concatenate([far_up, far_down])[None]
    east = dp_move(near, 0, 1)
    west = dp_move(near, 0, -1)
    east_far = dp_move(far, 0, 1)
    west_far = dp_move(far, 0, -1)
    two_east = dp_move(east[:2], 0, 1)
    two_west = dp_move(jnp.concatenate([west[2:], west_far]), 0, -1)
    return near, far, east, east_far, west, west_far, two_east, two_west


W_PIECES = ((0, 0), (0, 3), (3, 0), (3, 3), (1, 0), (1, 3), (2, 0), (2, 2))
ZH_REL = (0, 3, 1, 2)


def forward_kernel(idx_ref, x_ref, *refs):
    w_refs, (out_ref, head_ref, x_buf, w_buf, x_sem, w_sem) = refs[:8], refs[8:]
    blocks, rows, depth = x_ref.shape
    for block in range(blocks):
        pltpu.make_async_copy(
            x_ref.at[block], x_buf.at[:, block * depth : (block + 1) * depth], x_sem.at[block]
        ).start()
    for piece, ref in enumerate(w_refs):
        rel, first = W_PIECES[piece]
        for k in range(ref.shape[0]):
            slot = lax.rem(idx_ref[0] + ZH_REL[first + k], 4) * 4 + lax.rem(idx_ref[1] + rel, 4)
            pltpu.make_async_copy(ref.at[k], w_buf.at[slot], w_sem.at[slot]).start()
    total = jnp.zeros((rows, w_buf.shape[2]), F32)
    for part in range(4):
        for block in range(8 * part, 8 * part + 8):
            pltpu.make_async_copy(
                x_ref.at[0], x_buf.at[:, block * depth : (block + 1) * depth], x_sem.at[block]
            ).wait()
        for slot in range(4 * part, 4 * part + 4):
            pltpu.make_async_copy(w_refs[0].at[0], w_buf.at[slot], w_sem.at[slot]).wait()
        weights = w_buf[4 * part : 4 * part + 4].reshape(8 * depth, w_buf.shape[2])
        total = total + jnp.dot(
            x_buf[:, 8 * part * depth : 8 * (part + 1) * depth],
            weights,
            preferred_element_type=F32,
        )
    turned = total.T.astype(BF)
    out_ref[...] = turned
    half = turned.shape[1] // 2
    head_ref[:, :128] = turned[:, :128]
    head_ref[:, 128:] = turned[:, half : half + 128]


def forward_matmul(idx, features, panels):
    blocks, rows, depth = features.shape
    width = panels[0].shape[2]
    return pl.pallas_call(
        forward_kernel,
        out_shape=[
            jax.ShapeDtypeStruct((width, rows), BF),
            jax.ShapeDtypeStruct((width, 256), BF),
        ],
        in_specs=[
            pl.BlockSpec(memory_space=pltpu.SMEM),
            pl.BlockSpec(memory_space=pltpu.HBM),
        ]
        + [pl.BlockSpec(memory_space=pl.ANY)] * 8,
        out_specs=[pl.BlockSpec(memory_space=pltpu.VMEM)] * 2,
        scratch_shapes=[
            pltpu.VMEM((rows, blocks * depth), BF),
            pltpu.VMEM((blocks // 2, 2 * depth, width), BF),
            pltpu.SemaphoreType.DMA((blocks,)),
            pltpu.SemaphoreType.DMA((blocks // 2,)),
        ],
        compiler_params=pltpu.CompilerParams(vmem_limit_bytes=40 << 20),
    )(idx, features, *panels)


GROUPS = ((2,), (1, 3, 0))
HALF = 128
SMALL = 32


def split(value):
    high = value.astype(BF)
    return high, (value - high.astype(F32)).astype(BF)


def joined(message):
    return message[:, :128].astype(F32) + message[:, 128:256].astype(F32)


def put_small(ref, first, value):
    high, rest = split(value)
    ref[first : first + SMALL, 0:128] = high
    ref[first : first + SMALL, 128:256] = rest
    ref[first : first + SMALL, 256:512] = jnp.zeros((SMALL, 256), BF)


def ring_sum(own, before, after, opposite):
    high, rest = split(own)
    return (high.astype(F32) + rest.astype(F32) + joined(opposite)) + (joined(before) + joined(after))


def small_rows(value):
    return jnp.concatenate([*split(value), jnp.zeros((SMALL, 256), BF)], axis=1)


def backward_kernel(rels, idx_ref, x_ref, grad_ref, *refs):
    east, west, keep_e, keep_w, own, x_buf, x_sem = refs[-7:]
    count, depth = len(rels), x_buf.shape[2]
    order = [(rel_x, k, rel) for rel_x in (2, 1, 3, 0) for k, rel in enumerate(rels)]
    copies = []
    for place, (rel_x, _, rel) in enumerate(order):
        slot = lax.rem(idx_ref[0] + rel, 4) * 8 + lax.rem(idx_ref[1] + rel_x, 4) * 2
        copy = pltpu.make_async_copy(
            x_ref.at[pl.ds(slot, 2)], x_buf.at[pl.ds(2 * place, 2)], x_sem.at[place]
        )
        copy.start()
        copies.append(copy)
    if count == 1:
        for ref in (east, west):
            put_small(ref, 2 * HALF, refs[0][...])
    grad = grad_ref[...]
    for place, (rel_x, k, _) in enumerate(order):
        first = slice(k * HALF, (k + 1) * HALF)
        second = slice((count + k) * HALF, (count + k + 1) * HALF)
        low_to, high_to = {
            2: ((east, first), (west, first)),
            1: ((keep_e, first), (east, second)),
            3: ((west, second), (keep_w, first)),
            0: ((own, first), (own, second)),
        }[rel_x]
        copies[place].wait()
        for core in range(2):
            columns = slice(core * depth, (core + 1) * depth)
            part = jnp.dot(grad, x_buf[2 * place + core], preferred_element_type=F32).astype(BF)
            low_to[0][low_to[1], columns] = part[:HALF]
            high_to[0][high_to[1], columns] = part[HALF:]


def backward_matmul(rels, idx, features, grad, *small):
    _, rows, depth = features.shape
    count = len(rels)
    one = jax.ShapeDtypeStruct((count * HALF, 2 * depth), BF)
    two = jax.ShapeDtypeStruct((2 * count * HALF, 2 * depth), BF)
    sent = jax.ShapeDtypeStruct((2 * count * HALF + SMALL * len(small), 2 * depth), BF)
    return pl.pallas_call(
        functools.partial(backward_kernel, rels),
        out_shape=[sent, sent, one, one, two],
        in_specs=[
            pl.BlockSpec(memory_space=pltpu.SMEM),
            pl.BlockSpec(memory_space=pltpu.HBM),
        ]
        + [pl.BlockSpec(memory_space=pltpu.VMEM)] * (1 + len(small)),
        out_specs=[pl.BlockSpec(memory_space=pltpu.VMEM)] * 5,
        scratch_shapes=[
            pltpu.VMEM((8 * count, rows, depth), BF),
            pltpu.SemaphoreType.DMA((4 * count,)),
        ],
        compiler_params=pltpu.CompilerParams(vmem_limit_bytes=40 << 20),
    )(idx, features, grad, *small)


def add(*terms):
    total = terms[0].astype(F32)
    for term in terms[1:]:
        total = total + term.astype(F32)
    return total


def ring_first(parts):
    return dp_move(parts[0], 0, 1), dp_move(parts[1], 0, -1)


def ring_second(parts, received):
    _, _, keep_e, keep_w, _ = parts
    from_west, from_east = received
    rows = keep_e.shape[0]
    east = add(keep_e, from_west[:rows]).astype(BF)
    west = add(keep_w, from_east[:rows]).astype(BF)
    if from_west.shape[0] > 2 * rows:
        east = jnp.concatenate([east, from_west[2 * rows :]])
    return dp_move(east, 0, 1), dp_move(west, 0, -1)


def reduce_grads(idx, features, outgoing, small):
    far = backward_matmul(GROUPS[0], idx, features, outgoing, small)
    from_west, from_east = far_first = ring_first(far)
    near = backward_matmul(GROUPS[1], idx, features, outgoing)
    near_first = ring_first(near)
    east2, west2 = ring_second(far, far_first)
    low = add(far[4][:HALF], from_east[HALF : 2 * HALF], east2[:HALF]).astype(BF)
    high = add(far[4][HALF:], from_west[HALF : 2 * HALF], west2).astype(BF)
    small = ring_sum(small, from_west[2 * HALF :], from_east[2 * HALF :], east2[HALF:])
    row = small_rows(small)
    from_south = dp_move(jnp.concatenate([low, row]), 1, 0)
    from_north = dp_move(jnp.concatenate([high, row]), -1, 0)
    east2, west2 = ring_second(near, near_first)
    from_west, from_east = near_first
    low = add(near[4][: 3 * HALF], from_east[3 * HALF :], east2)
    high = add(near[4][3 * HALF :], from_west[3 * HALF :], west2)
    north = jnp.concatenate(
        [
            add(low[:HALF], from_south[:HALF]).astype(BF),
            high[:HALF].astype(BF),
            from_south[HALF:],
        ]
    )
    south = jnp.concatenate(
        [low[HALF : 2 * HALF].astype(BF), add(high[HALF : 2 * HALF], from_north[:HALF]).astype(BF)]
    )
    north2, south2 = dp_move(north, 1, 0), dp_move(south, -1, 0)
    small = ring_sum(small, from_south[HALF:], from_north[HALF:], north2[2 * HALF :])
    key = add(low[2 * HALF :], north2[:HALF], south2[:HALF]).astype(BF).T
    value = add(high[2 * HALF :], north2[HALF : 2 * HALF], south2[HALF:]).astype(BF).T
    return key, value, small


def toeplitz(row):
    spread = jnp.broadcast_to(row, (256, 256))
    return pltpu.roll(spread, 0, 1, stride=1, stride_axis=0)[:, :128].astype(BF)


def cotangent_kernel(meta_ref, own_ref, next_ref, ahead_ref, behind_ref, up_ref, grad_ref, band_ref, ext):
    for s in range(2):
        base = meta_ref[0]
        place = lax.broadcasted_iota(jnp.int32, (128, 256), 1) + base
        own = own_ref[s].astype(F32).T
        own = jnp.where(place < meta_ref[1 + s], own, 0.0).astype(BF)
        up_ref[:, s * 256 : (s + 1) * 256] = own
        tail = jnp.concatenate([next_ref[s].astype(F32), jnp.zeros((112, 128), F32)]).T
        tail = jnp.where(place + 256 < meta_ref[1 + s], tail, 0.0).astype(BF)
        ext[:, s * 512 : s * 512 + 256] = own
        ext[:, s * 512 + 256 : (s + 1) * 512] = tail
    for g in range(8):
        band_ref[g] = toeplitz(behind_ref[g : g + 1])
        rows = slice(16 * g, 16 * g + 16)
        left = jnp.concatenate(
            [
                ext[rows, s * 512 + 128 * b : s * 512 + 128 * b + 256]
                for s in range(2)
                for b in range(3)
            ]
        )
        total = jnp.dot(left, toeplitz(ahead_ref[g : g + 1]), preferred_element_type=F32)
        for part in range(6):
            grad_ref[rows, part * 128 : part * 128 + 128] = total[part * 16 : part * 16 + 16]


def cotangent_terms(meta, own, after, medium):
    zeros = jnp.zeros((8, 128), F32)
    ahead = jnp.concatenate([medium[:, :1], zeros, medium[:, :0:-1]], axis=1)
    behind = jnp.concatenate([zeros, medium], axis=1)
    return pl.pallas_call(
        cotangent_kernel,
        out_shape=[
            jax.ShapeDtypeStruct((128, 512), BF),
            jax.ShapeDtypeStruct((128, 768), F32),
            jax.ShapeDtypeStruct((8, 256, 128), BF),
        ],
        in_specs=[pl.BlockSpec(memory_space=pltpu.SMEM)] + [pl.BlockSpec(memory_space=pltpu.VMEM)] * 4,
        out_specs=[pl.BlockSpec(memory_space=pltpu.VMEM)] * 3,
        scratch_shapes=[pltpu.VMEM((128, 1024), BF)],
    )(meta, own, after, ahead, behind)


def middle_kernel(
    kv_ref, prev_ref, head_ref, grad_ref, taps_ref, dy_ref, prod_ref, sums_ref
):
    lanes = lax.broadcasted_iota(jnp.int32, (128, 128), 1)
    sums = jnp.zeros((128, 128), F32)
    partial = [[None] * 7 for _ in range(2)]
    for s in range(2):
        smooth = []
        for b in range(2):
            rows = slice(128 * b, 128 * b + 128)
            ext = jnp.concatenate(
                [
                    prev_ref[rows, s * 256 : (s + 1) * 256],
                    kv_ref[rows, s * 256 : (s + 1) * 256],
                    head_ref[rows, s * 128 : (s + 1) * 128],
                ],
                axis=1,
            ).astype(F32)
            total = taps_ref[rows, 0:1] * ext
            for j in range(1, 7):
                total = total + taps_ref[rows, j : j + 1] * pltpu.roll(ext, j, 1)
            smooth.append(total[:, 128:])
        prod_ref[:, s * 384 : (s + 1) * 384] = (smooth[0][:, :384] * smooth[1][:, :384]).astype(BF)
        for b in range(2):
            rows = slice(128 * b, 128 * b + 128)
            slope = grad_ref[:, s * 384 : (s + 1) * 384] * smooth[1 - b][:, 128:512]
            own = kv_ref[rows, s * 256 : (s + 1) * 256].astype(F32)
            act = jnp.zeros((128, 256), F32)
            for j in range(7):
                moved = (slope if j == 0 else pltpu.roll(slope, 384 - j, 1))[:, :256]
                act = act + taps_ref[rows, j : j + 1] * moved
                both = moved * own
                both = both[:, :128] + both[:, 128:]
                partial[b][j] = both if s == 0 else partial[b][j] + both
            dy_ref[rows, s * 256 : (s + 1) * 256] = act.astype(BF)
    for b in range(2):
        for j in range(7):
            column = jnp.sum(partial[b][j], axis=1, keepdims=True)
            sums = jnp.where(lanes == b * 8 + j, column, sums)
    sums_ref[...] = sums.T[0:16]


def middle_terms(kv, prev, head, grad, short_filters):
    taps = jnp.pad(short_filters.reshape(256, 7), ((0, 0), (0, 1)))
    return pl.pallas_call(
        middle_kernel,
        out_shape=[
            jax.ShapeDtypeStruct((256, 512), BF),
            jax.ShapeDtypeStruct((128, 768), BF),
            jax.ShapeDtypeStruct((16, 128), F32),
        ],
        in_specs=[pl.BlockSpec(memory_space=pltpu.VMEM)] * 5,
        out_specs=[pl.BlockSpec(memory_space=pltpu.VMEM)] * 3,
    )(kv, prev, head, grad, taps)


def response_kernel(meta_ref, prod, up_ref, band_ref, sums_ref, mixed_ref, small_ref, resp):
    small_ref[0:16] = sums_ref[...]
    for g in range(8):
        rows = slice(16 * g, 16 * g + 16)
        left = jnp.concatenate(
            [
                prod[rows, s * 384 + 128 * b : s * 384 + 128 * b + 256]
                for s in range(2)
                for b in range(2)
            ]
        )
        total = jnp.dot(left, band_ref[g], preferred_element_type=F32)
        for part in range(4):
            resp[rows, part * 128 : part * 128 + 128] = total[part * 16 : part * 16 + 16]
        above = jnp.concatenate(
            [up_ref[rows, part * 128 : part * 128 + 128] for part in range(4)]
        )
        folded = lax.dot_general(
            above, left, (((0,), (0,)), ((), ())), preferred_element_type=F32
        )
        count = 64
        while count >= 1:
            folded = folded[:count] + pltpu.roll(folded[count : 2 * count], 256 - count, 1)
            count //= 2
        small_ref[16 + g : 17 + g] = folded[:, :128]
        small_ref[24 + g : 25 + g] = folded[:, 128:]
    for s in range(2):
        place = lax.broadcasted_iota(jnp.int32, (256, 128), 0) + meta_ref[0]
        turned = resp[:, s * 256 : (s + 1) * 256].T
        mixed_ref[s] = jnp.where(place < meta_ref[1 + s], turned, 0.0).astype(BF)


def response_terms(meta, prod, up, bands, sums):
    return pl.pallas_call(
        response_kernel,
        out_shape=[
            jax.ShapeDtypeStruct((2, 256, 128), BF),
            jax.ShapeDtypeStruct((32, 128), F32),
        ],
        in_specs=[pl.BlockSpec(memory_space=pltpu.SMEM)] + [pl.BlockSpec(memory_space=pltpu.VMEM)] * 4,
        out_specs=[pl.BlockSpec(memory_space=pltpu.VMEM)] * 2,
        scratch_shapes=[pltpu.VMEM((128, 512), F32)],
    )(meta, prod, up, bands, sums)


def body(inputs, key_panel, value_panel, short_filters, medium_filters, lengths, cotangent):
    seqs, count, local_width = inputs.shape
    channels = key_panel.shape[1]
    dp = lax.axis_index("dp")
    idx = jnp.stack([dp // 4, dp % 4]).astype(jnp.int32)
    meta = jnp.concatenate([(dp * count).reshape(1).astype(jnp.int32), lengths])

    features = lax.all_gather(inputs.reshape(seqs * count, local_width), "shard", axis=0)
    features = pltpu.with_memory_space_constraint(features, pltpu.HBM)
    panels = gather_panels(jnp.concatenate([key_panel, value_panel], axis=1))
    after = shifted(cotangent[:, :144], -1)
    up, product_grad, bands = cotangent_terms(meta, cotangent, after, medium_filters)

    kv, head = forward_matmul(idx, features, panels)
    prev = shifted(kv, 1)
    head = shifted(head, -1)
    outgoing, product, sums = middle_terms(kv, prev, head, product_grad, short_filters)

    mixed, small = response_terms(meta, product, up, bands, sums)
    key_grad, value_grad, small = reduce_grads(idx, features, outgoing, small)
    short_grad = small[:16].reshape(2, 8, channels)[:, :7].transpose(0, 2, 1)
    medium_grad = jnp.concatenate([small[24:, :1], small[16:24, :0:-1]], axis=1)
    return (mixed, key_grad, value_grad, short_grad, medium_grad)


def solution(mesh):
    return jax.shard_map(
        body,
        mesh=mesh,
        in_specs=(
            P(None, "dp", "shard"),
            P("dp", "shard"),
            P("dp", "shard"),
            P(None, "shard", None),
            P("shard", None),
            P(),
            P(None, "dp", "shard"),
        ),
        out_specs=(
            P(None, "dp", "shard"),
            P("dp", "shard"),
            P("dp", "shard"),
            P(None, "shard", None),
            P("shard", None),
        ),
        check_vma=False,
    )
```

```python
import functools

import jax
import jax.numpy as jnp
from jax import lax
from jax.experimental import pallas as pl
from jax.experimental.pallas import tpu as pltpu
from jax.sharding import PartitionSpec as P


BF = jnp.bfloat16
F32 = jnp.float32


def dp_move(value, dzh, dx):
    pairs = [
        (zh * 4 + x, ((zh + dzh) % 4) * 4 + (x + dx) % 4) for zh in range(4) for x in range(4)
    ]
    return lax.ppermute(value, "dp", pairs)


def shifted(value, steps):
    first, last = (max(0, -steps), min(16, 16 - steps))
    return lax.ppermute(value, "dp", [(i, i + steps) for i in range(first, last)])


def gather_panels(block):
    half = block.shape[0] // 2
    up = dp_move(block, 1, 0)
    down = dp_move(block, -1, 0)
    far_up = dp_move(up[:half], 1, 0)
    far_down = dp_move(down[half:], -1, 0)
    near = jnp.stack([block, up, down])
    far = jnp.concatenate([far_up, far_down])[None]
    east = dp_move(near, 0, 1)
    west = dp_move(near, 0, -1)
    east_far = dp_move(far, 0, 1)
    west_far = dp_move(far, 0, -1)
    two_east = dp_move(east[:2], 0, 1)
    two_west = dp_move(jnp.concatenate([west[2:], west_far]), 0, -1)
    return near, far, east, east_far, west, west_far, two_east, two_west


W_PIECES = ((0, 0), (0, 3), (3, 0), (3, 3), (1, 0), (1, 3), (2, 0), (2, 2))
ZH_REL = (0, 3, 1, 2)


def forward_kernel(idx_ref, x_ref, taps_ref, *refs):
    w_refs, (out_ref, prev_ref, head_ref, x_buf, w_buf, x_sem, w_sem) = refs[:8], refs[8:]
    blocks, rows, depth = x_ref.shape
    width, half = w_buf.shape[2], rows // 2
    for block in range(blocks):
        pltpu.make_async_copy(
            x_ref.at[block], x_buf.at[:, block * depth : (block + 1) * depth], x_sem.at[block]
        ).start()
    for piece, ref in enumerate(w_refs):
        rel, first = W_PIECES[piece]
        for k in range(ref.shape[0]):
            slot = lax.rem(idx_ref[0] + ZH_REL[first + k], 4) * 4 + lax.rem(idx_ref[1] + rel, 4)
            pltpu.make_async_copy(ref.at[k], w_buf.at[slot], w_sem.at[slot]).start()
    totals = [jnp.zeros((half, width), F32) for _ in range(2)]
    for part in range(4):
        for block in range(8 * part, 8 * part + 8):
            pltpu.make_async_copy(
                x_ref.at[0], x_buf.at[:, block * depth : (block + 1) * depth], x_sem.at[block]
            ).wait()
        for slot in range(4 * part, 4 * part + 4):
            pltpu.make_async_copy(w_refs[0].at[0], w_buf.at[slot], w_sem.at[slot]).wait()
        weights = w_buf[4 * part : 4 * part + 4].reshape(8 * depth, width)
        for s in range(2):
            totals[s] = totals[s] + jnp.dot(
                x_buf[s * half : (s + 1) * half, 8 * part * depth : 8 * (part + 1) * depth],
                weights,
                preferred_element_type=F32,
            )
    head_ref[...] = jnp.concatenate([total[:8] for total in totals]).astype(BF)
    prev_ref[128:] = jnp.concatenate([total[half - 8 :] for total in totals]).astype(BF)
    for s in range(2):
        turned = totals[s].T.astype(BF)
        out_ref[:, s * half : (s + 1) * half] = turned
        smooth = []
        for b in range(2):
            branch = slice(128 * b, 128 * b + 128)
            smooth.append(short_smooth(turned[branch].astype(F32), taps_ref, branch)[:, half - 128 :])
        prev_ref[:128, s * 128 : (s + 1) * 128] = (smooth[0] * smooth[1]).astype(BF)


def short_smooth(ext, taps_ref, rows):
    total = taps_ref[rows, 0:1] * ext
    for j in range(1, 7):
        total = total + taps_ref[rows, j : j + 1] * pltpu.roll(ext, j, 1)
    return total


def forward_matmul(idx, features, taps, panels):
    blocks, rows, depth = features.shape
    width = panels[0].shape[2]
    return pl.pallas_call(
        forward_kernel,
        out_shape=[
            jax.ShapeDtypeStruct((width, rows), BF),
            jax.ShapeDtypeStruct((144, width), BF),
            jax.ShapeDtypeStruct((16, width), BF),
        ],
        in_specs=[
            pl.BlockSpec(memory_space=pltpu.SMEM),
            pl.BlockSpec(memory_space=pltpu.HBM),
            pl.BlockSpec(memory_space=pltpu.VMEM),
        ]
        + [pl.BlockSpec(memory_space=pl.ANY)] * 8,
        out_specs=[pl.BlockSpec(memory_space=pltpu.VMEM)] * 3,
        scratch_shapes=[
            pltpu.VMEM((rows, blocks * depth), BF),
            pltpu.VMEM((blocks // 2, 2 * depth, width), BF),
            pltpu.SemaphoreType.DMA((blocks,)),
            pltpu.SemaphoreType.DMA((blocks // 2,)),
        ],
        compiler_params=pltpu.CompilerParams(vmem_limit_bytes=40 << 20),
    )(idx, features, taps, *panels)


GROUPS = ((2,), (1, 3, 0))
HALF = 128
SMALL = 32


def split(value):
    high = value.astype(BF)
    return high, (value - high.astype(F32)).astype(BF)


def joined(message):
    return message[:, :128].astype(F32) + message[:, 128:256].astype(F32)


def put_small(ref, first, value):
    high, rest = split(value)
    ref[first : first + SMALL, 0:128] = high
    ref[first : first + SMALL, 128:256] = rest
    ref[first : first + SMALL, 256:512] = jnp.zeros((SMALL, 256), BF)


def ring_sum(own, before, after, opposite):
    high, rest = split(own)
    return (high.astype(F32) + rest.astype(F32) + joined(opposite)) + (joined(before) + joined(after))


def small_rows(value):
    return jnp.concatenate([*split(value), jnp.zeros((SMALL, 256), BF)], axis=1)


def backward_kernel(rels, idx_ref, x_ref, grad_ref, *refs):
    east, west, keep_e, keep_w, own, x_buf, x_sem = refs[-7:]
    count, depth = len(rels), x_buf.shape[2]
    order = [(rel_x, k, rel) for rel_x in (2, 1, 3, 0) for k, rel in enumerate(rels)]
    copies = []
    for place, (rel_x, _, rel) in enumerate(order):
        slot = lax.rem(idx_ref[0] + rel, 4) * 8 + lax.rem(idx_ref[1] + rel_x, 4) * 2
        copy = pltpu.make_async_copy(
            x_ref.at[pl.ds(slot, 2)], x_buf.at[pl.ds(2 * place, 2)], x_sem.at[place]
        )
        copy.start()
        copies.append(copy)
    if count == 1:
        for ref in (east, west):
            put_small(ref, 2 * HALF, refs[0][...])
    grad = grad_ref[...]
    for place, (rel_x, k, _) in enumerate(order):
        first = slice(k * HALF, (k + 1) * HALF)
        second = slice((count + k) * HALF, (count + k + 1) * HALF)
        low_to, high_to = {
            2: ((east, first), (west, first)),
            1: ((keep_e, first), (east, second)),
            3: ((west, second), (keep_w, first)),
            0: ((own, first), (own, second)),
        }[rel_x]
        copies[place].wait()
        for core in range(2):
            columns = slice(core * depth, (core + 1) * depth)
            part = jnp.dot(grad, x_buf[2 * place + core], preferred_element_type=F32).astype(BF)
            low_to[0][low_to[1], columns] = part[:HALF]
            high_to[0][high_to[1], columns] = part[HALF:]


def backward_matmul(rels, idx, features, grad, *small):
    _, rows, depth = features.shape
    count = len(rels)
    one = jax.ShapeDtypeStruct((count * HALF, 2 * depth), BF)
    two = jax.ShapeDtypeStruct((2 * count * HALF, 2 * depth), BF)
    sent = jax.ShapeDtypeStruct((2 * count * HALF + SMALL * len(small), 2 * depth), BF)
    return pl.pallas_call(
        functools.partial(backward_kernel, rels),
        out_shape=[sent, sent, one, one, two],
        in_specs=[
            pl.BlockSpec(memory_space=pltpu.SMEM),
            pl.BlockSpec(memory_space=pltpu.HBM),
        ]
        + [pl.BlockSpec(memory_space=pltpu.VMEM)] * (1 + len(small)),
        out_specs=[pl.BlockSpec(memory_space=pltpu.VMEM)] * 5,
        scratch_shapes=[
            pltpu.VMEM((8 * count, rows, depth), BF),
            pltpu.SemaphoreType.DMA((4 * count,)),
        ],
        compiler_params=pltpu.CompilerParams(vmem_limit_bytes=40 << 20),
    )(idx, features, grad, *small)


def add(*terms):
    total = terms[0].astype(F32)
    for term in terms[1:]:
        total = total + term.astype(F32)
    return total


def ring_first(parts):
    return dp_move(parts[0], 0, 1), dp_move(parts[1], 0, -1)


def ring_second(parts, received):
    _, _, keep_e, keep_w, _ = parts
    from_west, from_east = received
    rows = keep_e.shape[0]
    east = add(keep_e, from_west[:rows]).astype(BF)
    west = add(keep_w, from_east[:rows]).astype(BF)
    if from_west.shape[0] > 2 * rows:
        east = jnp.concatenate([east, from_west[2 * rows :]])
    return dp_move(east, 0, 1), dp_move(west, 0, -1)


def reduce_grads(idx, features, outgoing, small):
    far = backward_matmul(GROUPS[0], idx, features, outgoing, small)
    from_west, from_east = far_first = ring_first(far)
    near = backward_matmul(GROUPS[1], idx, features, outgoing)
    near_first = ring_first(near)
    east2, west2 = ring_second(far, far_first)
    low = add(far[4][:HALF], from_east[HALF : 2 * HALF], east2[:HALF]).astype(BF)
    high = add(far[4][HALF:], from_west[HALF : 2 * HALF], west2).astype(BF)
    small = ring_sum(small, from_west[2 * HALF :], from_east[2 * HALF :], east2[HALF:])
    row = small_rows(small)
    from_south = dp_move(jnp.concatenate([low, row]), 1, 0)
    from_north = dp_move(jnp.concatenate([high, row]), -1, 0)
    east2, west2 = ring_second(near, near_first)
    from_west, from_east = near_first
    low = add(near[4][: 3 * HALF], from_east[3 * HALF :], east2)
    high = add(near[4][3 * HALF :], from_west[3 * HALF :], west2)
    north = jnp.concatenate(
        [
            add(low[:HALF], from_south[:HALF]).astype(BF),
            high[:HALF].astype(BF),
            from_south[HALF:],
        ]
    )
    south = jnp.concatenate(
        [low[HALF : 2 * HALF].astype(BF), add(high[HALF : 2 * HALF], from_north[:HALF]).astype(BF)]
    )
    north2, south2 = dp_move(north, 1, 0), dp_move(south, -1, 0)
    small = ring_sum(small, from_south[HALF:], from_north[HALF:], north2[2 * HALF :])
    key = add(low[2 * HALF :], north2[:HALF], south2[:HALF]).astype(BF).T
    value = add(high[2 * HALF :], north2[HALF : 2 * HALF], south2[HALF:]).astype(BF).T
    return key, value, small


def toeplitz(row):
    spread = jnp.broadcast_to(row, (256, 256))
    return pltpu.roll(spread, 0, 1, stride=1, stride_axis=0)[:, :128].astype(BF)


def cotangent_kernel(meta_ref, own_ref, next_ref, ahead_ref, behind_ref, up_ref, grad_ref, band_ref, ext):
    for s in range(2):
        base = meta_ref[0]
        place = lax.broadcasted_iota(jnp.int32, (128, 256), 1) + base
        own = own_ref[s].astype(F32).T
        own = jnp.where(place < meta_ref[1 + s], own, 0.0).astype(BF)
        up_ref[:, s * 256 : (s + 1) * 256] = own
        tail = jnp.concatenate([next_ref[s].astype(F32), jnp.zeros((112, 128), F32)]).T
        tail = jnp.where(place + 256 < meta_ref[1 + s], tail, 0.0).astype(BF)
        ext[:, s * 512 : s * 512 + 256] = own
        ext[:, s * 512 + 256 : (s + 1) * 512] = tail
    for g in range(8):
        band_ref[g] = toeplitz(behind_ref[g : g + 1])
        rows = slice(16 * g, 16 * g + 16)
        left = jnp.concatenate(
            [
                ext[rows, s * 512 + 128 * b : s * 512 + 128 * b + 256]
                for s in range(2)
                for b in range(3)
            ]
        )
        total = jnp.dot(left, toeplitz(ahead_ref[g : g + 1]), preferred_element_type=F32)
        for part in range(6):
            grad_ref[rows, part * 128 : part * 128 + 128] = total[part * 16 : part * 16 + 16]


def cotangent_terms(meta, own, after, medium):
    zeros = jnp.zeros((8, 128), F32)
    ahead = jnp.concatenate([medium[:, :1], zeros, medium[:, :0:-1]], axis=1)
    behind = jnp.concatenate([zeros, medium], axis=1)
    return pl.pallas_call(
        cotangent_kernel,
        out_shape=[
            jax.ShapeDtypeStruct((128, 512), BF),
            jax.ShapeDtypeStruct((128, 768), F32),
            jax.ShapeDtypeStruct((8, 256, 128), BF),
        ],
        in_specs=[pl.BlockSpec(memory_space=pltpu.SMEM)] + [pl.BlockSpec(memory_space=pltpu.VMEM)] * 4,
        out_specs=[pl.BlockSpec(memory_space=pltpu.VMEM)] * 3,
        scratch_shapes=[pltpu.VMEM((128, 1024), BF)],
    )(meta, own, after, ahead, behind)


def middle_kernel(
    kv_ref, prev_ref, head_ref, grad_ref, taps_ref, dy_ref, prod_ref, sums_ref
):
    lanes = lax.broadcasted_iota(jnp.int32, (128, 128), 1)
    sums = jnp.zeros((128, 128), F32)
    partial = [[None] * 7 for _ in range(2)]
    zeros = jnp.zeros((112, 256), F32)
    before = jnp.concatenate([prev_ref[128:].astype(F32), zeros]).T
    after = jnp.concatenate([head_ref[...].astype(F32), zeros]).T
    for s in range(2):
        smooth = []
        for b in range(2):
            rows = slice(128 * b, 128 * b + 128)
            ext = jnp.concatenate(
                [
                    pltpu.roll(before[rows], 120 - 8 * s, 1),
                    kv_ref[rows, s * 256 : (s + 1) * 256].astype(F32),
                    after[rows] if s == 0 else pltpu.roll(after[rows], 120, 1),
                ],
                axis=1,
            )
            smooth.append(short_smooth(ext, taps_ref, rows)[:, 128:])
        prod_ref[:, s * 384 : s * 384 + 128] = prev_ref[:128, s * 128 : (s + 1) * 128]
        prod_ref[:, s * 384 + 128 : (s + 1) * 384] = (
            smooth[0][:, :256] * smooth[1][:, :256]
        ).astype(BF)
        for b in range(2):
            rows = slice(128 * b, 128 * b + 128)
            slope = grad_ref[:, s * 384 : (s + 1) * 384] * smooth[1 - b]
            own = kv_ref[rows, s * 256 : (s + 1) * 256].astype(F32)
            act = jnp.zeros((128, 256), F32)
            for j in range(7):
                moved = (slope if j == 0 else pltpu.roll(slope, 384 - j, 1))[:, :256]
                act = act + taps_ref[rows, j : j + 1] * moved
                both = moved * own
                both = both[:, :128] + both[:, 128:]
                partial[b][j] = both if s == 0 else partial[b][j] + both
            dy_ref[rows, s * 256 : (s + 1) * 256] = act.astype(BF)
    for b in range(2):
        for j in range(7):
            column = jnp.sum(partial[b][j], axis=1, keepdims=True)
            sums = jnp.where(lanes == b * 8 + j, column, sums)
    sums_ref[...] = sums.T[0:16]


def middle_terms(kv, prev, head, grad, taps):
    return pl.pallas_call(
        middle_kernel,
        out_shape=[
            jax.ShapeDtypeStruct((256, 512), BF),
            jax.ShapeDtypeStruct((128, 768), BF),
            jax.ShapeDtypeStruct((16, 128), F32),
        ],
        in_specs=[pl.BlockSpec(memory_space=pltpu.VMEM)] * 5,
        out_specs=[pl.BlockSpec(memory_space=pltpu.VMEM)] * 3,
    )(kv, prev, head, grad, taps)


def response_kernel(meta_ref, prod, up_ref, band_ref, sums_ref, mixed_ref, small_ref, resp):
    small_ref[0:16] = sums_ref[...]
    for g in range(8):
        rows = slice(16 * g, 16 * g + 16)
        left = jnp.concatenate(
            [
                prod[rows, s * 384 + 128 * b : s * 384 + 128 * b + 256]
                for s in range(2)
                for b in range(2)
            ]
        )
        total = jnp.dot(left, band_ref[g], preferred_element_type=F32)
        for part in range(4):
            resp[rows, part * 128 : part * 128 + 128] = total[part * 16 : part * 16 + 16]
        above = jnp.concatenate(
            [up_ref[rows, part * 128 : part * 128 + 128] for part in range(4)]
        )
        folded = lax.dot_general(
            above, left, (((0,), (0,)), ((), ())), preferred_element_type=F32
        )
        count = 64
        while count >= 1:
            folded = folded[:count] + pltpu.roll(folded[count : 2 * count], 256 - count, 1)
            count //= 2
        small_ref[16 + g : 17 + g] = folded[:, :128]
        small_ref[24 + g : 25 + g] = folded[:, 128:]
    for s in range(2):
        place = lax.broadcasted_iota(jnp.int32, (256, 128), 0) + meta_ref[0]
        turned = resp[:, s * 256 : (s + 1) * 256].T
        mixed_ref[s] = jnp.where(place < meta_ref[1 + s], turned, 0.0).astype(BF)


def response_terms(meta, prod, up, bands, sums):
    return pl.pallas_call(
        response_kernel,
        out_shape=[
            jax.ShapeDtypeStruct((2, 256, 128), BF),
            jax.ShapeDtypeStruct((32, 128), F32),
        ],
        in_specs=[pl.BlockSpec(memory_space=pltpu.SMEM)] + [pl.BlockSpec(memory_space=pltpu.VMEM)] * 4,
        out_specs=[pl.BlockSpec(memory_space=pltpu.VMEM)] * 2,
        scratch_shapes=[pltpu.VMEM((128, 512), F32)],
    )(meta, prod, up, bands, sums)


def body(inputs, key_panel, value_panel, short_filters, medium_filters, lengths, cotangent):
    seqs, count, local_width = inputs.shape
    channels = key_panel.shape[1]
    dp = lax.axis_index("dp")
    idx = jnp.stack([dp // 4, dp % 4]).astype(jnp.int32)
    meta = jnp.concatenate([(dp * count).reshape(1).astype(jnp.int32), lengths])

    features = lax.all_gather(inputs.reshape(seqs * count, local_width), "shard", axis=0)
    features = pltpu.with_memory_space_constraint(features, pltpu.HBM)
    panels = gather_panels(jnp.concatenate([key_panel, value_panel], axis=1))
    after = shifted(cotangent[:, :144], -1)
    up, product_grad, bands = cotangent_terms(meta, cotangent, after, medium_filters)

    taps = jnp.pad(short_filters.reshape(256, 7), ((0, 0), (0, 1)))
    kv, prev, head = forward_matmul(idx, features, taps, panels)
    prev = shifted(prev, 1)
    head = shifted(head, -1)
    outgoing, product, sums = middle_terms(kv, prev, head, product_grad, taps)

    mixed, small = response_terms(meta, product, up, bands, sums)
    key_grad, value_grad, small = reduce_grads(idx, features, outgoing, small)
    short_grad = small[:16].reshape(2, 8, channels)[:, :7].transpose(0, 2, 1)
    medium_grad = jnp.concatenate([small[24:, :1], small[16:24, :0:-1]], axis=1)
    return (mixed, key_grad, value_grad, short_grad, medium_grad)


def solution(mesh):
    return jax.shard_map(
        body,
        mesh=mesh,
        in_specs=(
            P(None, "dp", "shard"),
            P("dp", "shard"),
            P("dp", "shard"),
            P(None, "shard", None),
            P("shard", None),
            P(),
            P(None, "dp", "shard"),
        ),
        out_specs=(
            P(None, "dp", "shard"),
            P("dp", "shard"),
            P("dp", "shard"),
            P(None, "shard", None),
            P("shard", None),
        ),
        check_vma=False,
    )
```

```python
import functools

import jax
import jax.numpy as jnp
from jax import lax
from jax.experimental import pallas as pl
from jax.experimental.pallas import tpu as pltpu
from jax.sharding import PartitionSpec as P


BF = jnp.bfloat16
F32 = jnp.float32


def in_hbm(value):
    return pltpu.with_memory_space_constraint(value, pltpu.HBM)


def dp_move(value, dzh, dx):
    pairs = [
        (zh * 4 + x, ((zh + dzh) % 4) * 4 + (x + dx) % 4) for zh in range(4) for x in range(4)
    ]
    return lax.ppermute(value, "dp", pairs)


def shifted(value, steps):
    first, last = (max(0, -steps), min(16, 16 - steps))
    return lax.ppermute(value, "dp", [(i, i + steps) for i in range(first, last)])


def gather_panels(block):
    half = block.shape[0] // 2
    up = dp_move(block, 1, 0)
    down = dp_move(block, -1, 0)
    far_up = dp_move(up[:half], 1, 0)
    far_down = dp_move(down[half:], -1, 0)
    near = jnp.stack([block, up, down])
    far = jnp.concatenate([far_up, far_down])[None]
    east = dp_move(near, 0, 1)
    west = dp_move(near, 0, -1)
    east_far = dp_move(far, 0, 1)
    west_far = dp_move(far, 0, -1)
    two_east = dp_move(east[:2], 0, 1)
    two_west = dp_move(jnp.concatenate([west[2:], west_far]), 0, -1)
    return near, far, east, east_far, west, west_far, two_east, two_west


W_PIECES = ((0, 0), (0, 3), (3, 0), (3, 3), (1, 0), (1, 3), (2, 0), (2, 2))
ZH_REL = (0, 3, 1, 2)


def forward_kernel(idx_ref, x_ref, taps_ref, *refs):
    w_refs, (out_ref, prev_ref, head_ref, x_buf, w_buf, x_sem, w_sem) = refs[:8], refs[8:]
    blocks, rows, depth = x_ref.shape
    width, half = w_buf.shape[2], rows // 2
    for block in range(blocks):
        pltpu.make_async_copy(
            x_ref.at[block], x_buf.at[:, block * depth : (block + 1) * depth], x_sem.at[block]
        ).start()
    for piece, ref in enumerate(w_refs):
        rel, first = W_PIECES[piece]
        for k in range(ref.shape[0]):
            slot = lax.rem(idx_ref[0] + ZH_REL[first + k], 4) * 4 + lax.rem(idx_ref[1] + rel, 4)
            pltpu.make_async_copy(ref.at[k], w_buf.at[slot], w_sem.at[slot]).start()
    totals = [jnp.zeros((half, width), F32) for _ in range(2)]
    for part in range(4):
        for block in range(8 * part, 8 * part + 8):
            pltpu.make_async_copy(
                x_ref.at[0], x_buf.at[:, block * depth : (block + 1) * depth], x_sem.at[block]
            ).wait()
        for slot in range(4 * part, 4 * part + 4):
            pltpu.make_async_copy(w_refs[0].at[0], w_buf.at[slot], w_sem.at[slot]).wait()
        weights = w_buf[4 * part : 4 * part + 4].reshape(8 * depth, width)
        for s in range(2):
            totals[s] = totals[s] + jnp.dot(
                x_buf[s * half : (s + 1) * half, 8 * part * depth : 8 * (part + 1) * depth],
                weights,
                preferred_element_type=F32,
            )
    head_ref[...] = jnp.concatenate([total[:8] for total in totals]).astype(BF)
    prev_ref[128:] = jnp.concatenate([total[half - 8 :] for total in totals]).astype(BF)
    for s in range(2):
        turned = totals[s].T.astype(BF)
        out_ref[:, s * half : (s + 1) * half] = turned
        smooth = []
        for b in range(2):
            branch = slice(128 * b, 128 * b + 128)
            smooth.append(short_smooth(turned[branch].astype(F32), taps_ref, branch)[:, half - 128 :])
        prev_ref[:128, s * 128 : (s + 1) * 128] = (smooth[0] * smooth[1]).astype(BF)


def short_smooth(ext, taps_ref, rows):
    total = taps_ref[rows, 0:1] * ext
    for j in range(1, 7):
        total = total + taps_ref[rows, j : j + 1] * pltpu.roll(ext, j, 1)
    return total


def forward_matmul(idx, features, taps, panels):
    blocks, rows, depth = features.shape
    width = panels[0].shape[2]
    return pl.pallas_call(
        forward_kernel,
        out_shape=[
            jax.ShapeDtypeStruct((width, rows), BF),
            jax.ShapeDtypeStruct((144, width), BF),
            jax.ShapeDtypeStruct((16, width), BF),
        ],
        in_specs=[
            pl.BlockSpec(memory_space=pltpu.SMEM),
            pl.BlockSpec(memory_space=pltpu.HBM),
            pl.BlockSpec(memory_space=pltpu.VMEM),
        ]
        + [pl.BlockSpec(memory_space=pl.ANY)] * 8,
        out_specs=[pl.BlockSpec(memory_space=pltpu.VMEM)] * 3,
        scratch_shapes=[
            pltpu.VMEM((rows, blocks * depth), BF),
            pltpu.VMEM((blocks // 2, 2 * depth, width), BF),
            pltpu.SemaphoreType.DMA((blocks,)),
            pltpu.SemaphoreType.DMA((blocks // 2,)),
        ],
        compiler_params=pltpu.CompilerParams(vmem_limit_bytes=40 << 20),
    )(idx, features, taps, *panels)


GROUPS = ((2,), (1, 3, 0))
HALF = 128
SMALL = 32


def split(value):
    high = value.astype(BF)
    return high, (value - high.astype(F32)).astype(BF)


def joined(message):
    return message[:, :128].astype(F32) + message[:, 128:256].astype(F32)


def put_small(ref, first, value):
    high, rest = split(value)
    ref[first : first + SMALL, 0:128] = high
    ref[first : first + SMALL, 128:256] = rest
    ref[first : first + SMALL, 256:512] = jnp.zeros((SMALL, 256), BF)


def ring_sum(own, before, after, opposite):
    high, rest = split(own)
    return (high.astype(F32) + rest.astype(F32) + joined(opposite)) + (joined(before) + joined(after))


def small_rows(value):
    return jnp.concatenate([*split(value), jnp.zeros((SMALL, 256), BF)], axis=1)


def backward_kernel(rels, idx_ref, x_ref, grad_ref, *refs):
    east, west, keep_e, keep_w, own, x_buf, x_sem = refs[-7:]
    count, depth = len(rels), x_buf.shape[2]
    order = [(rel_x, k, rel) for rel_x in (2, 1, 3, 0) for k, rel in enumerate(rels)]
    copies = []
    for place, (rel_x, _, rel) in enumerate(order):
        slot = lax.rem(idx_ref[0] + rel, 4) * 8 + lax.rem(idx_ref[1] + rel_x, 4) * 2
        copy = pltpu.make_async_copy(
            x_ref.at[pl.ds(slot, 2)], x_buf.at[pl.ds(2 * place, 2)], x_sem.at[place]
        )
        copy.start()
        copies.append(copy)
    if count == 1:
        for ref in (east, west):
            put_small(ref, 2 * HALF, refs[0][...])
    grad = grad_ref[...]
    for place, (rel_x, k, _) in enumerate(order):
        first = slice(k * HALF, (k + 1) * HALF)
        second = slice((count + k) * HALF, (count + k + 1) * HALF)
        low_to, high_to = {
            2: ((east, first), (west, first)),
            1: ((keep_e, first), (east, second)),
            3: ((west, second), (keep_w, first)),
            0: ((own, first), (own, second)),
        }[rel_x]
        copies[place].wait()
        for core in range(2):
            columns = slice(core * depth, (core + 1) * depth)
            part = jnp.dot(grad, x_buf[2 * place + core], preferred_element_type=F32).astype(BF)
            low_to[0][low_to[1], columns] = part[:HALF]
            high_to[0][high_to[1], columns] = part[HALF:]


def backward_matmul(rels, idx, features, grad, *small):
    _, rows, depth = features.shape
    count = len(rels)
    one = jax.ShapeDtypeStruct((count * HALF, 2 * depth), BF)
    two = jax.ShapeDtypeStruct((2 * count * HALF, 2 * depth), BF)
    sent = jax.ShapeDtypeStruct((2 * count * HALF + SMALL * len(small), 2 * depth), BF)
    return pl.pallas_call(
        functools.partial(backward_kernel, rels),
        out_shape=[sent, sent, one, one, two],
        in_specs=[
            pl.BlockSpec(memory_space=pltpu.SMEM),
            pl.BlockSpec(memory_space=pltpu.HBM),
        ]
        + [pl.BlockSpec(memory_space=pltpu.VMEM)] * (1 + len(small)),
        out_specs=[pl.BlockSpec(memory_space=pltpu.VMEM)] * 5,
        scratch_shapes=[
            pltpu.VMEM((8 * count, rows, depth), BF),
            pltpu.SemaphoreType.DMA((4 * count,)),
        ],
        compiler_params=pltpu.CompilerParams(vmem_limit_bytes=40 << 20),
    )(idx, features, grad, *small)


def add(*terms):
    total = terms[0].astype(F32)
    for term in terms[1:]:
        total = total + term.astype(F32)
    return total


def ring_first(parts):
    return dp_move(parts[0], 0, 1), dp_move(parts[1], 0, -1)


def ring_second(parts, received):
    _, _, keep_e, keep_w, _ = parts
    from_west, from_east = received
    rows = keep_e.shape[0]
    east = add(keep_e, from_west[:rows]).astype(BF)
    west = add(keep_w, from_east[:rows]).astype(BF)
    if from_west.shape[0] > 2 * rows:
        east = jnp.concatenate([east, from_west[2 * rows :]])
    return dp_move(east, 0, 1), dp_move(west, 0, -1)


def reduce_grads(idx, features, outgoing, small):
    far = backward_matmul(GROUPS[0], idx, features, outgoing, in_hbm(small))
    from_west, from_east = far_first = ring_first(far)
    near = backward_matmul(GROUPS[1], idx, features, outgoing)
    near_first = ring_first(near)
    east2, west2 = ring_second(far, far_first)
    from_west, from_east = lax.optimization_barrier((from_west, from_east))
    low = add(far[4][:HALF], from_east[HALF : 2 * HALF], east2[:HALF]).astype(BF)
    high = add(far[4][HALF:], from_west[HALF : 2 * HALF], west2).astype(BF)
    small = ring_sum(small, from_west[2 * HALF :], from_east[2 * HALF :], east2[HALF:])
    low = jnp.concatenate([low, small_rows(small)])
    high = jnp.concatenate([high, small_rows(small)])
    from_south = dp_move(low, 1, 0)
    from_north = dp_move(high, -1, 0)
    east2, west2 = ring_second(near, near_first)
    from_west, from_east = near_first
    low = add(near[4][: 3 * HALF], from_east[3 * HALF :], east2)
    high = add(near[4][3 * HALF :], from_west[3 * HALF :], west2)
    north = jnp.concatenate(
        [
            add(low[:HALF], from_south[:HALF]).astype(BF),
            high[:HALF].astype(BF),
            from_south[HALF:],
        ]
    )
    south = jnp.concatenate(
        [low[HALF : 2 * HALF].astype(BF), add(high[HALF : 2 * HALF], from_north[:HALF]).astype(BF)]
    )
    north2, south2 = dp_move(north, 1, 0), dp_move(south, -1, 0)
    small = ring_sum(small, from_south[HALF:], from_north[HALF:], north2[2 * HALF :])
    key = add(low[2 * HALF :], north2[:HALF], south2[:HALF]).astype(BF).T
    value = add(high[2 * HALF :], north2[HALF : 2 * HALF], south2[HALF:]).astype(BF).T
    return key, value, small


def toeplitz(row):
    spread = jnp.broadcast_to(row, (256, 256))
    return pltpu.roll(spread, 0, 1, stride=1, stride_axis=0)[:, :128].astype(BF)


def cotangent_kernel(meta_ref, own_ref, next_ref, ahead_ref, behind_ref, up_ref, grad_ref, band_ref, ext):
    for s in range(2):
        base = meta_ref[0]
        place = lax.broadcasted_iota(jnp.int32, (128, 256), 1) + base
        own = own_ref[s].astype(F32).T
        own = jnp.where(place < meta_ref[1 + s], own, 0.0).astype(BF)
        up_ref[:, s * 256 : (s + 1) * 256] = own
        tail = jnp.concatenate([next_ref[s].astype(F32), jnp.zeros((112, 128), F32)]).T
        tail = jnp.where(place + 256 < meta_ref[1 + s], tail, 0.0).astype(BF)
        ext[:, s * 512 : s * 512 + 256] = own
        ext[:, s * 512 + 256 : (s + 1) * 512] = tail
    for g in range(8):
        band_ref[g] = toeplitz(behind_ref[g : g + 1])
        rows = slice(16 * g, 16 * g + 16)
        left = jnp.concatenate(
            [
                ext[rows, s * 512 + 128 * b : s * 512 + 128 * b + 256]
                for s in range(2)
                for b in range(3)
            ]
        )
        total = jnp.dot(left, toeplitz(ahead_ref[g : g + 1]), preferred_element_type=F32)
        for part in range(6):
            grad_ref[rows, part * 128 : part * 128 + 128] = total[part * 16 : part * 16 + 16]


def cotangent_terms(meta, own, after, medium):
    zeros = jnp.zeros((8, 128), F32)
    ahead = jnp.concatenate([medium[:, :1], zeros, medium[:, :0:-1]], axis=1)
    behind = jnp.concatenate([zeros, medium], axis=1)
    return pl.pallas_call(
        cotangent_kernel,
        out_shape=[
            jax.ShapeDtypeStruct((128, 512), BF),
            jax.ShapeDtypeStruct((128, 768), F32),
            jax.ShapeDtypeStruct((8, 256, 128), BF),
        ],
        in_specs=[pl.BlockSpec(memory_space=pltpu.SMEM)] + [pl.BlockSpec(memory_space=pltpu.VMEM)] * 4,
        out_specs=[pl.BlockSpec(memory_space=pltpu.VMEM)] * 3,
        scratch_shapes=[pltpu.VMEM((128, 1024), BF)],
    )(meta, own, after, ahead, behind)


def middle_kernel(
    kv_ref, prev_ref, head_ref, grad_ref, taps_ref, dy_ref, prod_ref, sums_ref
):
    lanes = lax.broadcasted_iota(jnp.int32, (128, 128), 1)
    sums = jnp.zeros((128, 128), F32)
    partial = [[None] * 7 for _ in range(2)]
    zeros = jnp.zeros((112, 256), F32)
    before = jnp.concatenate([prev_ref[128:].astype(F32), zeros]).T
    after = jnp.concatenate([head_ref[...].astype(F32), zeros]).T
    for s in range(2):
        smooth = []
        for b in range(2):
            rows = slice(128 * b, 128 * b + 128)
            ext = jnp.concatenate(
                [
                    pltpu.roll(before[rows], 120 - 8 * s, 1),
                    kv_ref[rows, s * 256 : (s + 1) * 256].astype(F32),
                    after[rows] if s == 0 else pltpu.roll(after[rows], 120, 1),
                ],
                axis=1,
            )
            smooth.append(short_smooth(ext, taps_ref, rows)[:, 128:])
        prod_ref[:, s * 384 : s * 384 + 128] = prev_ref[:128, s * 128 : (s + 1) * 128]
        prod_ref[:, s * 384 + 128 : (s + 1) * 384] = (
            smooth[0][:, :256] * smooth[1][:, :256]
        ).astype(BF)
        for b in range(2):
            rows = slice(128 * b, 128 * b + 128)
            slope = grad_ref[:, s * 384 : (s + 1) * 384] * smooth[1 - b]
            own = kv_ref[rows, s * 256 : (s + 1) * 256].astype(F32)
            act = jnp.zeros((128, 256), F32)
            for j in range(7):
                moved = (slope if j == 0 else pltpu.roll(slope, 384 - j, 1))[:, :256]
                act = act + taps_ref[rows, j : j + 1] * moved
                both = moved * own
                both = both[:, :128] + both[:, 128:]
                partial[b][j] = both if s == 0 else partial[b][j] + both
            dy_ref[rows, s * 256 : (s + 1) * 256] = act.astype(BF)
    for b in range(2):
        for j in range(7):
            column = jnp.sum(partial[b][j], axis=1, keepdims=True)
            sums = jnp.where(lanes == b * 8 + j, column, sums)
    sums_ref[...] = sums.T[0:16]


def middle_terms(kv, prev, head, grad, taps):
    return pl.pallas_call(
        middle_kernel,
        out_shape=[
            jax.ShapeDtypeStruct((256, 512), BF),
            jax.ShapeDtypeStruct((128, 768), BF),
            jax.ShapeDtypeStruct((16, 128), F32),
        ],
        in_specs=[pl.BlockSpec(memory_space=pltpu.VMEM)] * 5,
        out_specs=[pl.BlockSpec(memory_space=pltpu.VMEM)] * 3,
    )(kv, prev, head, grad, taps)


def response_kernel(meta_ref, prod, up_ref, band_ref, sums_ref, mixed_ref, small_ref, resp):
    small_ref[0:16] = sums_ref[...]
    for g in range(8):
        rows = slice(16 * g, 16 * g + 16)
        left = jnp.concatenate(
            [
                prod[rows, s * 384 + 128 * b : s * 384 + 128 * b + 256]
                for s in range(2)
                for b in range(2)
            ]
        )
        total = jnp.dot(left, band_ref[g], preferred_element_type=F32)
        for part in range(4):
            resp[rows, part * 128 : part * 128 + 128] = total[part * 16 : part * 16 + 16]
        above = jnp.concatenate(
            [up_ref[rows, part * 128 : part * 128 + 128] for part in range(4)]
        )
        folded = lax.dot_general(
            above, left, (((0,), (0,)), ((), ())), preferred_element_type=F32
        )
        count = 64
        while count >= 1:
            folded = folded[:count] + pltpu.roll(folded[count : 2 * count], 256 - count, 1)
            count //= 2
        small_ref[16 + g : 17 + g] = folded[:, :128]
        small_ref[24 + g : 25 + g] = folded[:, 128:]
    for s in range(2):
        place = lax.broadcasted_iota(jnp.int32, (256, 128), 0) + meta_ref[0]
        turned = resp[:, s * 256 : (s + 1) * 256].T
        mixed_ref[s] = jnp.where(place < meta_ref[1 + s], turned, 0.0).astype(BF)


def response_terms(meta, prod, up, bands, sums):
    return pl.pallas_call(
        response_kernel,
        out_shape=[
            jax.ShapeDtypeStruct((2, 256, 128), BF),
            jax.ShapeDtypeStruct((32, 128), F32),
        ],
        in_specs=[pl.BlockSpec(memory_space=pltpu.SMEM)] + [pl.BlockSpec(memory_space=pltpu.VMEM)] * 4,
        out_specs=[pl.BlockSpec(memory_space=pltpu.VMEM)] * 2,
        scratch_shapes=[pltpu.VMEM((128, 512), F32)],
    )(meta, prod, up, bands, sums)


def body(inputs, key_panel, value_panel, short_filters, medium_filters, lengths, cotangent):
    seqs, count, local_width = inputs.shape
    channels = key_panel.shape[1]
    dp = lax.axis_index("dp")
    idx = jnp.stack([dp // 4, dp % 4]).astype(jnp.int32)
    meta = jnp.concatenate([(dp * count).reshape(1).astype(jnp.int32), lengths])

    features = lax.all_gather(inputs.reshape(seqs * count, local_width), "shard", axis=0)
    features = in_hbm(features)
    panels = gather_panels(jnp.concatenate([key_panel, value_panel], axis=1))
    after = shifted(cotangent[:, :144], -1)
    up, product_grad, bands = cotangent_terms(meta, cotangent, after, medium_filters)

    taps = jnp.pad(short_filters.reshape(256, 7), ((0, 0), (0, 1)))
    kv, prev, head = forward_matmul(idx, features, taps, panels)
    prev = in_hbm(shifted(prev, 1))
    head = in_hbm(shifted(head, -1))
    outgoing, product, sums = middle_terms(in_hbm(kv), prev, head, product_grad, taps)
    outgoing = in_hbm(outgoing)
    mixed, small = response_terms(meta, product, up, bands, sums)
    key_grad, value_grad, small = reduce_grads(idx, features, outgoing, small)
    short_grad = small[:16].reshape(2, 8, channels)[:, :7].transpose(0, 2, 1)
    medium_grad = jnp.concatenate([small[24:, :1], small[16:24, :0:-1]], axis=1)
    return (mixed, key_grad, value_grad, short_grad, medium_grad)


def solution(mesh):
    return jax.shard_map(
        body,
        mesh=mesh,
        in_specs=(
            P(None, "dp", "shard"),
            P("dp", "shard"),
            P("dp", "shard"),
            P(None, "shard", None),
            P("shard", None),
            P(),
            P(None, "dp", "shard"),
        ),
        out_specs=(
            P(None, "dp", "shard"),
            P("dp", "shard"),
            P("dp", "shard"),
            P(None, "shard", None),
            P("shard", None),
        ),
        check_vma=False,
    )
```

```python
import functools

import jax
import jax.numpy as jnp
from jax import lax
from jax.experimental import pallas as pl
from jax.experimental.pallas import tpu as pltpu
from jax.sharding import PartitionSpec as P


BF = jnp.bfloat16
F32 = jnp.float32


def in_hbm(value):
    return pltpu.with_memory_space_constraint(value, pltpu.HBM)


def dp_move(value, dzh, dx):
    pairs = [
        (zh * 4 + x, ((zh + dzh) % 4) * 4 + (x + dx) % 4) for zh in range(4) for x in range(4)
    ]
    return lax.ppermute(value, "dp", pairs)


def dp_pairs(value, offset):
    pairs = [(i, i + 1) for i in range(offset, 15, 2)]
    return lax.ppermute(value, "dp", pairs + [(j, i) for i, j in pairs])


def shifted(value, steps):
    first, last = (max(0, -steps), min(16, 16 - steps))
    return lax.ppermute(value, "dp", [(i, i + steps) for i in range(first, last)])


def gather_panels(block):
    half = block.shape[0] // 2
    up = dp_move(block, 1, 0)
    down = dp_move(block, -1, 0)
    far_up = dp_move(up[:half], 1, 0)
    far_down = dp_move(down[half:], -1, 0)
    near = jnp.stack([block, up, down])
    far = jnp.concatenate([far_up, far_down])[None]
    east = dp_move(near, 0, 1)
    west = dp_move(near, 0, -1)
    east_far = dp_move(far, 0, 1)
    west_far = dp_move(far, 0, -1)
    two_east = dp_move(east[:2], 0, 1)
    two_west = dp_move(jnp.concatenate([west[2:], west_far]), 0, -1)
    return near, far, east, east_far, west, west_far, two_east, two_west


W_PIECES = ((0, 0), (0, 3), (3, 0), (3, 3), (1, 0), (1, 3), (2, 0), (2, 2))
ZH_REL = (0, 3, 1, 2)


def forward_kernel(idx_ref, x_ref, taps_ref, *refs):
    w_refs, (out_ref, edge_ref, x_buf, w_buf, x_sem, w_sem) = refs[:8], refs[8:]
    blocks, rows, depth = x_ref.shape
    width, half = w_buf.shape[2], rows // 2
    for piece, ref in enumerate(w_refs):
        rel, first = W_PIECES[piece]
        for k in range(ref.shape[0]):
            slot = lax.rem(idx_ref[0] + ZH_REL[first + k], 4) * 4 + lax.rem(idx_ref[1] + rel, 4)
            pltpu.make_async_copy(ref.at[k], w_buf.at[slot], w_sem.at[slot]).start()
    for block in range(blocks):
        pltpu.make_async_copy(
            x_ref.at[block], x_buf.at[:, block * depth : (block + 1) * depth], x_sem.at[block]
        ).start()
    totals = [jnp.zeros((half, width), F32) for _ in range(2)]
    for part in range(4):
        for block in range(8 * part, 8 * part + 8):
            pltpu.make_async_copy(
                x_ref.at[0], x_buf.at[:, block * depth : (block + 1) * depth], x_sem.at[block]
            ).wait()
        for slot in range(4 * part, 4 * part + 4):
            pltpu.make_async_copy(w_refs[0].at[0], w_buf.at[slot], w_sem.at[slot]).wait()
        weights = w_buf[4 * part : 4 * part + 4].reshape(8 * depth, width)
        for s in range(2):
            totals[s] = totals[s] + jnp.dot(
                x_buf[s * half : (s + 1) * half, 8 * part * depth : 8 * (part + 1) * depth],
                weights,
                preferred_element_type=F32,
            )
    edge_ref[128:144] = jnp.concatenate([total[half - 8 :] for total in totals]).astype(BF)
    edge_ref[144:160] = jnp.concatenate([total[:8] for total in totals]).astype(BF)
    for s in range(2):
        turned = totals[s].T.astype(BF)
        out_ref[:, s * half : (s + 1) * half] = turned
        smooth = []
        for b in range(2):
            branch = slice(128 * b, 128 * b + 128)
            smooth.append(short_smooth(turned[branch].astype(F32), taps_ref, branch)[:, half - 128 :])
        edge_ref[:128, s * 128 : (s + 1) * 128] = (smooth[0] * smooth[1]).astype(BF)


def short_smooth(ext, taps_ref, rows):
    total = taps_ref[rows, 0:1] * ext
    for j in range(1, 7):
        total = total + taps_ref[rows, j : j + 1] * pltpu.roll(ext, j, 1)
    return total


def forward_matmul(idx, features, taps, panels):
    blocks, rows, depth = features.shape
    width = panels[0].shape[2]
    return pl.pallas_call(
        forward_kernel,
        out_shape=[
            jax.ShapeDtypeStruct((width, rows), BF),
            jax.ShapeDtypeStruct((160, width), BF),
        ],
        in_specs=[
            pl.BlockSpec(memory_space=pltpu.SMEM),
            pl.BlockSpec(memory_space=pltpu.HBM),
            pl.BlockSpec(memory_space=pltpu.VMEM),
        ]
        + [pl.BlockSpec(memory_space=pl.ANY)] * 8,
        out_specs=[pl.BlockSpec(memory_space=pltpu.VMEM)] * 2,
        scratch_shapes=[
            pltpu.VMEM((rows, blocks * depth), BF),
            pltpu.VMEM((blocks // 2, 2 * depth, width), BF),
            pltpu.SemaphoreType.DMA((blocks,)),
            pltpu.SemaphoreType.DMA((blocks // 2,)),
        ],
        compiler_params=pltpu.CompilerParams(vmem_limit_bytes=40 << 20),
    )(idx, features, taps, *panels)


GROUPS = ((2,), (1, 3, 0))
HALF = 128
SMALL = 32


def split(value):
    high = value.astype(BF)
    return high, (value - high.astype(F32)).astype(BF)


def joined(message):
    return message[:, :128].astype(F32) + message[:, 128:256].astype(F32)


def put_small(ref, first, value):
    high, rest = split(value)
    ref[first : first + SMALL, 0:128] = high
    ref[first : first + SMALL, 128:256] = rest
    ref[first : first + SMALL, 256:512] = jnp.zeros((SMALL, 256), BF)


def ring_sum(own, before, after, opposite):
    high, rest = split(own)
    return (high.astype(F32) + rest.astype(F32) + joined(opposite)) + (joined(before) + joined(after))


def small_rows(value):
    return jnp.concatenate([*split(value), jnp.zeros((SMALL, 256), BF)], axis=1)


def backward_kernel(rels, idx_ref, x_ref, grad_ref, *refs):
    east, west, keep_e, keep_w, own, x_buf, x_sem = refs[-7:]
    count, depth = len(rels), x_buf.shape[2]
    order = [(rel_x, k, rel) for rel_x in (2, 1, 3, 0) for k, rel in enumerate(rels)]
    copies = []
    for place, (rel_x, _, rel) in enumerate(order):
        slot = lax.rem(idx_ref[0] + rel, 4) * 8 + lax.rem(idx_ref[1] + rel_x, 4) * 2
        copy = pltpu.make_async_copy(
            x_ref.at[pl.ds(slot, 2)], x_buf.at[pl.ds(2 * place, 2)], x_sem.at[place]
        )
        copy.start()
        copies.append(copy)
    if count == 1:
        for ref in (east, west):
            put_small(ref, 2 * HALF, refs[0][...])
    grad = grad_ref[...]
    for place, (rel_x, k, _) in enumerate(order):
        first = slice(k * HALF, (k + 1) * HALF)
        second = slice((count + k) * HALF, (count + k + 1) * HALF)
        low_to, high_to = {
            2: ((east, first), (west, first)),
            1: ((keep_e, first), (east, second)),
            3: ((west, second), (keep_w, first)),
            0: ((own, first), (own, second)),
        }[rel_x]
        copies[place].wait()
        for core in range(2):
            columns = slice(core * depth, (core + 1) * depth)
            part = jnp.dot(grad, x_buf[2 * place + core], preferred_element_type=F32).astype(BF)
            low_to[0][low_to[1], columns] = part[:HALF]
            high_to[0][high_to[1], columns] = part[HALF:]


def backward_matmul(rels, idx, features, grad, *small):
    _, rows, depth = features.shape
    count = len(rels)
    one = jax.ShapeDtypeStruct((count * HALF, 2 * depth), BF)
    two = jax.ShapeDtypeStruct((2 * count * HALF, 2 * depth), BF)
    sent = jax.ShapeDtypeStruct((2 * count * HALF + SMALL * len(small), 2 * depth), BF)
    return pl.pallas_call(
        functools.partial(backward_kernel, rels),
        out_shape=[sent, sent, one, one, two],
        in_specs=[
            pl.BlockSpec(memory_space=pltpu.SMEM),
            pl.BlockSpec(memory_space=pltpu.HBM),
        ]
        + [pl.BlockSpec(memory_space=pltpu.VMEM)] * (1 + len(small)),
        out_specs=[pl.BlockSpec(memory_space=pltpu.VMEM)] * 5,
        scratch_shapes=[
            pltpu.VMEM((8 * count, rows, depth), BF),
            pltpu.SemaphoreType.DMA((4 * count,)),
        ],
        compiler_params=pltpu.CompilerParams(vmem_limit_bytes=40 << 20),
    )(idx, features, grad, *small)


def add(*terms):
    total = terms[0].astype(F32)
    for term in terms[1:]:
        total = total + term.astype(F32)
    return total


def ring_first(parts):
    return dp_move(parts[0], 0, 1), dp_move(parts[1], 0, -1)


def ring_second(parts, received):
    _, _, keep_e, keep_w, _ = parts
    from_west, from_east = received
    rows = keep_e.shape[0]
    east = add(keep_e, from_west[:rows]).astype(BF)
    west = add(keep_w, from_east[:rows]).astype(BF)
    if from_west.shape[0] > 2 * rows:
        east = jnp.concatenate([east, from_west[2 * rows :]])
    return dp_move(east, 0, 1), dp_move(west, 0, -1)


def reduce_grads(idx, features, outgoing, small):
    far = backward_matmul(GROUPS[0], idx, features, outgoing, in_hbm(small))
    from_west, from_east = far_first = ring_first(far)
    near = backward_matmul(GROUPS[1], idx, features, outgoing)
    near_first = ring_first(near)
    east2, west2 = ring_second(far, far_first)
    from_west, from_east = lax.optimization_barrier((from_west, from_east))
    low = add(far[4][:HALF], from_east[HALF : 2 * HALF], east2[:HALF]).astype(BF)
    high = add(far[4][HALF:], from_west[HALF : 2 * HALF], west2).astype(BF)
    small = ring_sum(small, from_west[2 * HALF :], from_east[2 * HALF :], east2[HALF:])
    low = jnp.concatenate([low, small_rows(small)])
    high = jnp.concatenate([high, small_rows(small)])
    from_south = dp_move(low, 1, 0)
    from_north = dp_move(high, -1, 0)
    east2, west2 = ring_second(near, near_first)
    from_west, from_east = near_first
    low = add(near[4][: 3 * HALF], from_east[3 * HALF :], east2)
    high = add(near[4][3 * HALF :], from_west[3 * HALF :], west2)
    north = jnp.concatenate(
        [
            add(low[:HALF], from_south[:HALF]).astype(BF),
            high[:HALF].astype(BF),
            from_south[HALF:],
        ]
    )
    south = jnp.concatenate(
        [low[HALF : 2 * HALF].astype(BF), add(high[HALF : 2 * HALF], from_north[:HALF]).astype(BF)]
    )
    north2, south2 = dp_move(north, 1, 0), dp_move(south, -1, 0)
    small = ring_sum(small, from_south[HALF:], from_north[HALF:], north2[2 * HALF :])
    key = add(low[2 * HALF :], north2[:HALF], south2[:HALF]).astype(BF).T
    value = add(high[2 * HALF :], north2[HALF : 2 * HALF], south2[HALF:]).astype(BF).T
    return key, value, small


def toeplitz(row):
    spread = jnp.broadcast_to(row, (256, 256))
    return pltpu.roll(spread, 0, 1, stride=1, stride_axis=0)[:, :128].astype(BF)


def cotangent_kernel(meta_ref, own_ref, next_ref, ahead_ref, behind_ref, up_ref, grad_ref, band_ref, ext):
    for s in range(2):
        base = meta_ref[0]
        place = lax.broadcasted_iota(jnp.int32, (128, 256), 1) + base
        own = own_ref[s].astype(F32).T
        own = jnp.where(place < meta_ref[1 + s], own, 0.0).astype(BF)
        up_ref[:, s * 256 : (s + 1) * 256] = own
        tail = jnp.concatenate([next_ref[s].astype(F32), jnp.zeros((112, 128), F32)]).T
        tail = jnp.where(place + 256 < meta_ref[1 + s], tail, 0.0).astype(BF)
        ext[:, s * 512 : s * 512 + 256] = own
        ext[:, s * 512 + 256 : (s + 1) * 512] = tail
    for g in range(8):
        band_ref[g] = toeplitz(behind_ref[g : g + 1])
        rows = slice(16 * g, 16 * g + 16)
        left = jnp.concatenate(
            [
                ext[rows, s * 512 + 128 * b : s * 512 + 128 * b + 256]
                for s in range(2)
                for b in range(3)
            ]
        )
        total = jnp.dot(left, toeplitz(ahead_ref[g : g + 1]), preferred_element_type=F32)
        for part in range(6):
            grad_ref[rows, part * 128 : part * 128 + 128] = total[part * 16 : part * 16 + 16]


def cotangent_terms(meta, own, after, medium):
    zeros = jnp.zeros((8, 128), F32)
    ahead = jnp.concatenate([medium[:, :1], zeros, medium[:, :0:-1]], axis=1)
    behind = jnp.concatenate([zeros, medium], axis=1)
    return pl.pallas_call(
        cotangent_kernel,
        out_shape=[
            jax.ShapeDtypeStruct((128, 512), BF),
            jax.ShapeDtypeStruct((128, 768), F32),
            jax.ShapeDtypeStruct((8, 256, 128), BF),
        ],
        in_specs=[pl.BlockSpec(memory_space=pltpu.SMEM)] + [pl.BlockSpec(memory_space=pltpu.VMEM)] * 4,
        out_specs=[pl.BlockSpec(memory_space=pltpu.VMEM)] * 3,
        scratch_shapes=[pltpu.VMEM((128, 1024), BF)],
    )(meta, own, after, ahead, behind)


def middle_kernel(
    meta_ref, kv_ref, first_ref, second_ref, grad_ref, taps_ref, dy_ref, prod_ref, sums_ref
):
    lanes = lax.broadcasted_iota(jnp.int32, (128, 128), 1)
    sums = jnp.zeros((128, 128), F32)
    partial = [[None] * 7 for _ in range(2)]
    zeros = jnp.zeros((112, 256), F32)
    odd = meta_ref[3] == 1
    first, second = first_ref[...].astype(F32), second_ref[...].astype(F32)
    left, right = jnp.where(odd, first, second), jnp.where(odd, second, first)
    before = jnp.concatenate([left[128:144], zeros]).T
    after = jnp.concatenate([right[144:], zeros]).T
    for s in range(2):
        smooth = []
        for b in range(2):
            rows = slice(128 * b, 128 * b + 128)
            ext = jnp.concatenate(
                [
                    pltpu.roll(before[rows], 120 - 8 * s, 1),
                    kv_ref[rows, s * 256 : (s + 1) * 256].astype(F32),
                    after[rows] if s == 0 else pltpu.roll(after[rows], 120, 1),
                ],
                axis=1,
            )
            smooth.append(short_smooth(ext, taps_ref, rows)[:, 128:])
        prod_ref[:, s * 384 : s * 384 + 128] = left[:128, s * 128 : (s + 1) * 128].astype(BF)
        prod_ref[:, s * 384 + 128 : (s + 1) * 384] = (
            smooth[0][:, :256] * smooth[1][:, :256]
        ).astype(BF)
        for b in range(2):
            rows = slice(128 * b, 128 * b + 128)
            slope = grad_ref[:, s * 384 : (s + 1) * 384] * smooth[1 - b]
            own = kv_ref[rows, s * 256 : (s + 1) * 256].astype(F32)
            act = jnp.zeros((128, 256), F32)
            for j in range(7):
                moved = (slope if j == 0 else pltpu.roll(slope, 384 - j, 1))[:, :256]
                act = act + taps_ref[rows, j : j + 1] * moved
                both = moved * own
                both = both[:, :128] + both[:, 128:]
                partial[b][j] = both if s == 0 else partial[b][j] + both
            dy_ref[rows, s * 256 : (s + 1) * 256] = act.astype(BF)
    for b in range(2):
        for j in range(7):
            column = jnp.sum(partial[b][j], axis=1, keepdims=True)
            sums = jnp.where(lanes == b * 8 + j, column, sums)
    sums_ref[...] = sums.T[0:16]


def middle_terms(meta, kv, first, second, grad, taps):
    return pl.pallas_call(
        middle_kernel,
        out_shape=[
            jax.ShapeDtypeStruct((256, 512), BF),
            jax.ShapeDtypeStruct((128, 768), BF),
            jax.ShapeDtypeStruct((16, 128), F32),
        ],
        in_specs=[pl.BlockSpec(memory_space=pltpu.SMEM)] + [pl.BlockSpec(memory_space=pltpu.VMEM)] * 5,
        out_specs=[pl.BlockSpec(memory_space=pltpu.VMEM)] * 3,
    )(meta, kv, first, second, grad, taps)


def response_kernel(meta_ref, prod, up_ref, band_ref, sums_ref, mixed_ref, small_ref, resp):
    small_ref[0:16] = sums_ref[...]
    for g in range(8):
        rows = slice(16 * g, 16 * g + 16)
        left = jnp.concatenate(
            [
                prod[rows, s * 384 + 128 * b : s * 384 + 128 * b + 256]
                for s in range(2)
                for b in range(2)
            ]
        )
        total = jnp.dot(left, band_ref[g], preferred_element_type=F32)
        for part in range(4):
            resp[rows, part * 128 : part * 128 + 128] = total[part * 16 : part * 16 + 16]
        above = jnp.concatenate(
            [up_ref[rows, part * 128 : part * 128 + 128] for part in range(4)]
        )
        folded = lax.dot_general(
            above, left, (((0,), (0,)), ((), ())), preferred_element_type=F32
        )
        count = 64
        while count >= 1:
            folded = folded[:count] + pltpu.roll(folded[count : 2 * count], 256 - count, 1)
            count //= 2
        small_ref[16 + g : 17 + g] = folded[:, :128]
        small_ref[24 + g : 25 + g] = folded[:, 128:]
    for s in range(2):
        place = lax.broadcasted_iota(jnp.int32, (256, 128), 0) + meta_ref[0]
        turned = resp[:, s * 256 : (s + 1) * 256].T
        mixed_ref[s] = jnp.where(place < meta_ref[1 + s], turned, 0.0).astype(BF)


def response_terms(meta, prod, up, bands, sums):
    return pl.pallas_call(
        response_kernel,
        out_shape=[
            jax.ShapeDtypeStruct((2, 256, 128), BF),
            jax.ShapeDtypeStruct((32, 128), F32),
        ],
        in_specs=[pl.BlockSpec(memory_space=pltpu.SMEM)] + [pl.BlockSpec(memory_space=pltpu.VMEM)] * 4,
        out_specs=[pl.BlockSpec(memory_space=pltpu.VMEM)] * 2,
        scratch_shapes=[pltpu.VMEM((128, 512), F32)],
    )(meta, prod, up, bands, sums)


def body(inputs, key_panel, value_panel, short_filters, medium_filters, lengths, cotangent):
    seqs, count, local_width = inputs.shape
    channels = key_panel.shape[1]
    dp = lax.axis_index("dp")
    idx = jnp.stack([dp // 4, dp % 4]).astype(jnp.int32)
    meta = jnp.concatenate(
        [(dp * count).reshape(1).astype(jnp.int32), lengths, (dp % 2).reshape(1).astype(jnp.int32)]
    )

    features = lax.all_gather(inputs.reshape(seqs * count, local_width), "shard", axis=0)
    features = in_hbm(features)
    panels = gather_panels(jnp.concatenate([key_panel, value_panel], axis=1))
    after = shifted(cotangent[:, :144], -1)
    up, product_grad, bands = cotangent_terms(meta, cotangent, after, medium_filters)

    taps = jnp.pad(short_filters.reshape(256, 7), ((0, 0), (0, 1)))
    kv, edges = forward_matmul(idx, features, taps, panels)
    first = dp_pairs(edges, 0)
    second = dp_pairs(edges, 1)
    outgoing, product, sums = middle_terms(meta, in_hbm(kv), first, second, product_grad, taps)
    outgoing = in_hbm(outgoing)
    mixed, small = response_terms(meta, product, up, bands, sums)
    key_grad, value_grad, small = reduce_grads(idx, features, outgoing, small)
    short_grad = small[:16].reshape(2, 8, channels)[:, :7].transpose(0, 2, 1)
    medium_grad = jnp.concatenate([small[24:, :1], small[16:24, :0:-1]], axis=1)
    return (mixed, key_grad, value_grad, short_grad, medium_grad)


def solution(mesh):
    return jax.shard_map(
        body,
        mesh=mesh,
        in_specs=(
            P(None, "dp", "shard"),
            P("dp", "shard"),
            P("dp", "shard"),
            P(None, "shard", None),
            P("shard", None),
            P(),
            P(None, "dp", "shard"),
        ),
        out_specs=(
            P(None, "dp", "shard"),
            P("dp", "shard"),
            P("dp", "shard"),
            P(None, "shard", None),
            P("shard", None),
        ),
        check_vma=False,
    )
```

```python
import functools

import jax
import jax.numpy as jnp
from jax import lax
from jax.experimental import pallas as pl
from jax.experimental.pallas import tpu as pltpu
from jax.sharding import PartitionSpec as P


BF = jnp.bfloat16
F32 = jnp.float32


def in_hbm(value):
    return pltpu.with_memory_space_constraint(value, pltpu.HBM)


def dp_move(value, dzh, dx):
    pairs = [
        (zh * 4 + x, ((zh + dzh) % 4) * 4 + (x + dx) % 4) for zh in range(4) for x in range(4)
    ]
    return lax.ppermute(value, "dp", pairs)


def dp_pairs(value, offset):
    pairs = [(i, i + 1) for i in range(offset, 15, 2)]
    return lax.ppermute(value, "dp", pairs + [(j, i) for i, j in pairs])


def shifted(value, steps):
    first, last = (max(0, -steps), min(16, 16 - steps))
    return lax.ppermute(value, "dp", [(i, i + steps) for i in range(first, last)])


def gather_panels(block):
    half = block.shape[0] // 2
    up = dp_move(block, 1, 0)
    down = dp_move(block, -1, 0)
    far_up = dp_move(up[:half], 1, 0)
    far_down = dp_move(down[half:], -1, 0)
    near = jnp.stack([block, up, down])
    far = jnp.concatenate([far_up, far_down])[None]
    east = dp_move(near, 0, 1)
    west = dp_move(near, 0, -1)
    east_far = dp_move(far, 0, 1)
    west_far = dp_move(far, 0, -1)
    two_east = dp_move(east[:2], 0, 1)
    two_west = dp_move(jnp.concatenate([west[2:], west_far]), 0, -1)
    return near, far, east, east_far, west, west_far, two_east, two_west


W_PIECES = ((0, 0), (0, 3), (3, 0), (3, 3), (1, 0), (1, 3), (2, 0), (2, 2))
ZH_REL = (0, 3, 1, 2)


def forward_kernel(idx_ref, x_ref, taps_ref, *refs):
    w_refs, (out_ref, edge_ref, x_buf, w_buf, x_sem, w_sem) = refs[:8], refs[8:]
    blocks, rows, depth = x_ref.shape
    width, half = w_buf.shape[2], rows // 2
    for piece, ref in enumerate(w_refs):
        rel, first = W_PIECES[piece]
        for k in range(ref.shape[0]):
            slot = lax.rem(idx_ref[0] + ZH_REL[first + k], 4) * 4 + lax.rem(idx_ref[1] + rel, 4)
            pltpu.make_async_copy(ref.at[k], w_buf.at[slot], w_sem.at[slot]).start()
    for block in range(blocks):
        pltpu.make_async_copy(
            x_ref.at[block], x_buf.at[:, block * depth : (block + 1) * depth], x_sem.at[block]
        ).start()
    totals = [jnp.zeros((half, width), F32) for _ in range(2)]
    for part in range(4):
        for block in range(8 * part, 8 * part + 8):
            pltpu.make_async_copy(
                x_ref.at[0], x_buf.at[:, block * depth : (block + 1) * depth], x_sem.at[block]
            ).wait()
        for slot in range(4 * part, 4 * part + 4):
            pltpu.make_async_copy(w_refs[0].at[0], w_buf.at[slot], w_sem.at[slot]).wait()
        weights = w_buf[4 * part : 4 * part + 4].reshape(8 * depth, width)
        for s in range(2):
            totals[s] = totals[s] + jnp.dot(
                x_buf[s * half : (s + 1) * half, 8 * part * depth : 8 * (part + 1) * depth],
                weights,
                preferred_element_type=F32,
            )
    edge_ref[128:144] = jnp.concatenate([total[half - 8 :] for total in totals]).astype(BF)
    edge_ref[144:160] = jnp.concatenate([total[:8] for total in totals]).astype(BF)
    for s in range(2):
        turned = totals[s].T.astype(BF)
        out_ref[:, s * half : (s + 1) * half] = turned
        smooth = []
        for b in range(2):
            branch = slice(128 * b, 128 * b + 128)
            smooth.append(short_smooth(turned[branch].astype(F32), taps_ref, branch)[:, half - 128 :])
        edge_ref[:128, s * 128 : (s + 1) * 128] = (smooth[0] * smooth[1]).astype(BF)


def short_smooth(ext, taps_ref, rows):
    total = taps_ref[rows, 0:1] * ext
    for j in range(1, 7):
        total = total + taps_ref[rows, j : j + 1] * pltpu.roll(ext, j, 1)
    return total


def forward_matmul(idx, features, taps, panels):
    blocks, rows, depth = features.shape
    width = panels[0].shape[2]
    return pl.pallas_call(
        forward_kernel,
        out_shape=[
            jax.ShapeDtypeStruct((width, rows), BF),
            jax.ShapeDtypeStruct((160, width), BF),
        ],
        in_specs=[
            pl.BlockSpec(memory_space=pltpu.SMEM),
            pl.BlockSpec(memory_space=pltpu.HBM),
            pl.BlockSpec(memory_space=pltpu.VMEM),
        ]
        + [pl.BlockSpec(memory_space=pl.ANY)] * 8,
        out_specs=[pl.BlockSpec(memory_space=pltpu.VMEM)] * 2,
        scratch_shapes=[
            pltpu.VMEM((rows, blocks * depth), BF),
            pltpu.VMEM((blocks // 2, 2 * depth, width), BF),
            pltpu.SemaphoreType.DMA((blocks,)),
            pltpu.SemaphoreType.DMA((blocks // 2,)),
        ],
        compiler_params=pltpu.CompilerParams(vmem_limit_bytes=40 << 20),
    )(idx, features, taps, *panels)


GROUPS = ((2,), (1, 3, 0))
HALF = 128
SMALL = 16


def split(value):
    high = value.astype(BF)
    return high, (value - high.astype(F32)).astype(BF)


def narrow(rows):
    return jnp.concatenate([rows[:, 128 * q : 128 * q + 128] for q in range(4)]).astype(F32)


def wide(value):
    return jnp.concatenate([value[8 * q : 8 * q + 8] for q in range(4)], axis=1)


def joined(message):
    return narrow(message[:8]) + narrow(message[8:])


def put_small(ref, first, value):
    high = value.astype(BF).astype(F32)
    ref[first : first + SMALL] = jnp.concatenate([wide(high), wide(value - high)]).astype(BF)


def ring_sum(own, before, after, opposite):
    high, rest = split(own)
    return (high.astype(F32) + rest.astype(F32) + joined(opposite)) + (joined(before) + joined(after))


def small_rows(value):
    return jnp.concatenate([wide(part) for part in split(value)])


def backward_kernel(rels, idx_ref, x_ref, grad_ref, *refs):
    east, west, keep_e, keep_w, own, x_buf, x_sem = refs[-7:]
    count, depth = len(rels), x_buf.shape[2]
    order = [(rel_x, k, rel) for rel_x in (2, 1, 3, 0) for k, rel in enumerate(rels)]
    copies = []
    for place, (rel_x, _, rel) in enumerate(order):
        slot = lax.rem(idx_ref[0] + rel, 4) * 8 + lax.rem(idx_ref[1] + rel_x, 4) * 2
        copy = pltpu.make_async_copy(
            x_ref.at[pl.ds(slot, 2)], x_buf.at[pl.ds(2 * place, 2)], x_sem.at[place]
        )
        copy.start()
        copies.append(copy)
    if count == 1:
        for ref in (east, west):
            put_small(ref, 2 * HALF, refs[0][...])
    grad = grad_ref[...]
    for place, (rel_x, k, _) in enumerate(order):
        first = slice(k * HALF, (k + 1) * HALF)
        second = slice((count + k) * HALF, (count + k + 1) * HALF)
        low_to, high_to = {
            2: ((east, first), (west, first)),
            1: ((keep_e, first), (east, second)),
            3: ((west, second), (keep_w, first)),
            0: ((own, first), (own, second)),
        }[rel_x]
        copies[place].wait()
        for core in range(2):
            columns = slice(core * depth, (core + 1) * depth)
            part = jnp.dot(grad, x_buf[2 * place + core], preferred_element_type=F32).astype(BF)
            low_to[0][low_to[1], columns] = part[:HALF]
            high_to[0][high_to[1], columns] = part[HALF:]


def backward_matmul(rels, idx, features, grad, *small):
    _, rows, depth = features.shape
    count = len(rels)
    one = jax.ShapeDtypeStruct((count * HALF, 2 * depth), BF)
    two = jax.ShapeDtypeStruct((2 * count * HALF, 2 * depth), BF)
    sent = jax.ShapeDtypeStruct((2 * count * HALF + SMALL * len(small), 2 * depth), BF)
    return pl.pallas_call(
        functools.partial(backward_kernel, rels),
        out_shape=[sent, sent, one, one, two],
        in_specs=[
            pl.BlockSpec(memory_space=pltpu.SMEM),
            pl.BlockSpec(memory_space=pltpu.HBM),
        ]
        + [pl.BlockSpec(memory_space=pltpu.VMEM)] * (1 + len(small)),
        out_specs=[pl.BlockSpec(memory_space=pltpu.VMEM)] * 5,
        scratch_shapes=[
            pltpu.VMEM((8 * count, rows, depth), BF),
            pltpu.SemaphoreType.DMA((4 * count,)),
        ],
        compiler_params=pltpu.CompilerParams(vmem_limit_bytes=40 << 20),
    )(idx, features, grad, *small)


def add(*terms):
    total = terms[0].astype(F32)
    for term in terms[1:]:
        total = total + term.astype(F32)
    return total


def ring_first(parts):
    return dp_move(parts[0], 0, 1), dp_move(parts[1], 0, -1)


def ring_second(parts, received):
    _, _, keep_e, keep_w, _ = parts
    from_west, from_east = received
    rows = keep_e.shape[0]
    east = add(keep_e, from_west[:rows]).astype(BF)
    west = add(keep_w, from_east[:rows]).astype(BF)
    if from_west.shape[0] > 2 * rows:
        east = jnp.concatenate([east, from_west[2 * rows :]])
    return dp_move(east, 0, 1), dp_move(west, 0, -1)


def reduce_grads(idx, features, outgoing, small):
    far = backward_matmul(GROUPS[0], idx, features, outgoing, in_hbm(small))
    from_west, from_east = far_first = ring_first(far)
    near = backward_matmul(GROUPS[1], idx, features, outgoing)
    near_first = ring_first(near)
    east2, west2 = ring_second(far, far_first)
    from_west, from_east = lax.optimization_barrier((from_west, from_east))
    low = add(far[4][:HALF], from_east[HALF : 2 * HALF], east2[:HALF]).astype(BF)
    high = add(far[4][HALF:], from_west[HALF : 2 * HALF], west2).astype(BF)
    small = ring_sum(small, from_west[2 * HALF :], from_east[2 * HALF :], east2[HALF:])
    low = jnp.concatenate([low, small_rows(small)])
    high = jnp.concatenate([high, small_rows(small)])
    from_south = dp_move(low, 1, 0)
    from_north = dp_move(high, -1, 0)
    east2, west2 = ring_second(near, near_first)
    from_west, from_east = near_first
    low = add(near[4][: 3 * HALF], from_east[3 * HALF :], east2)
    high = add(near[4][3 * HALF :], from_west[3 * HALF :], west2)
    north = jnp.concatenate(
        [
            add(low[:HALF], from_south[:HALF]).astype(BF),
            high[:HALF].astype(BF),
            from_south[HALF:],
        ]
    )
    south = jnp.concatenate(
        [low[HALF : 2 * HALF].astype(BF), add(high[HALF : 2 * HALF], from_north[:HALF]).astype(BF)]
    )
    north2, south2 = dp_move(north, 1, 0), dp_move(south, -1, 0)
    small = ring_sum(small, from_south[HALF:], from_north[HALF:], north2[2 * HALF :])
    key = add(low[2 * HALF :], north2[:HALF], south2[:HALF]).astype(BF).T
    value = add(high[2 * HALF :], north2[HALF : 2 * HALF], south2[HALF:]).astype(BF).T
    return key, value, small


def toeplitz(row):
    spread = jnp.broadcast_to(row, (256, 256))
    return pltpu.roll(spread, 0, 1, stride=1, stride_axis=0)[:, :128].astype(BF)


def cotangent_kernel(meta_ref, own_ref, next_ref, ahead_ref, behind_ref, up_ref, grad_ref, band_ref, ext):
    for s in range(2):
        base = meta_ref[0]
        place = lax.broadcasted_iota(jnp.int32, (128, 256), 1) + base
        own = own_ref[s].astype(F32).T
        own = jnp.where(place < meta_ref[1 + s], own, 0.0).astype(BF)
        up_ref[:, s * 256 : (s + 1) * 256] = own
        tail = jnp.concatenate([next_ref[s].astype(F32), jnp.zeros((112, 128), F32)]).T
        tail = jnp.where(place + 256 < meta_ref[1 + s], tail, 0.0).astype(BF)
        ext[:, s * 512 : s * 512 + 256] = own
        ext[:, s * 512 + 256 : (s + 1) * 512] = tail
    for g in range(8):
        band_ref[g] = toeplitz(behind_ref[g : g + 1])
        rows = slice(16 * g, 16 * g + 16)
        left = jnp.concatenate(
            [
                ext[rows, s * 512 + 128 * b : s * 512 + 128 * b + 256]
                for s in range(2)
                for b in range(3)
            ]
        )
        total = jnp.dot(left, toeplitz(ahead_ref[g : g + 1]), preferred_element_type=F32)
        for part in range(6):
            grad_ref[rows, part * 128 : part * 128 + 128] = total[part * 16 : part * 16 + 16]


def cotangent_terms(meta, own, after, medium):
    zeros = jnp.zeros((8, 128), F32)
    ahead = jnp.concatenate([medium[:, :1], zeros, medium[:, :0:-1]], axis=1)
    behind = jnp.concatenate([zeros, medium], axis=1)
    return pl.pallas_call(
        cotangent_kernel,
        out_shape=[
            jax.ShapeDtypeStruct((128, 512), BF),
            jax.ShapeDtypeStruct((128, 768), F32),
            jax.ShapeDtypeStruct((8, 256, 128), BF),
        ],
        in_specs=[pl.BlockSpec(memory_space=pltpu.SMEM)] + [pl.BlockSpec(memory_space=pltpu.VMEM)] * 4,
        out_specs=[pl.BlockSpec(memory_space=pltpu.VMEM)] * 3,
        scratch_shapes=[pltpu.VMEM((128, 1024), BF)],
    )(meta, own, after, ahead, behind)


def middle_kernel(
    meta_ref, kv_ref, first_ref, second_ref, grad_ref, taps_ref, dy_ref, prod_ref, sums_ref
):
    lanes = lax.broadcasted_iota(jnp.int32, (128, 128), 1)
    sums = jnp.zeros((128, 128), F32)
    partial = [[None] * 7 for _ in range(2)]
    zeros = jnp.zeros((112, 256), F32)
    odd = meta_ref[3] == 1
    first, second = first_ref[...].astype(F32), second_ref[...].astype(F32)
    left, right = jnp.where(odd, first, second), jnp.where(odd, second, first)
    before = jnp.concatenate([left[128:144], zeros]).T
    after = jnp.concatenate([right[144:], zeros]).T
    for s in range(2):
        smooth = []
        for b in range(2):
            rows = slice(128 * b, 128 * b + 128)
            ext = jnp.concatenate(
                [
                    pltpu.roll(before[rows], 120 - 8 * s, 1),
                    kv_ref[rows, s * 256 : (s + 1) * 256].astype(F32),
                    after[rows] if s == 0 else pltpu.roll(after[rows], 120, 1),
                ],
                axis=1,
            )
            smooth.append(short_smooth(ext, taps_ref, rows)[:, 128:])
        prod_ref[:, s * 384 : s * 384 + 128] = left[:128, s * 128 : (s + 1) * 128].astype(BF)
        prod_ref[:, s * 384 + 128 : (s + 1) * 384] = (
            smooth[0][:, :256] * smooth[1][:, :256]
        ).astype(BF)
        for b in range(2):
            rows = slice(128 * b, 128 * b + 128)
            slope = grad_ref[:, s * 384 : (s + 1) * 384] * smooth[1 - b]
            own = kv_ref[rows, s * 256 : (s + 1) * 256].astype(F32)
            act = jnp.zeros((128, 256), F32)
            for j in range(7):
                moved = (slope if j == 0 else pltpu.roll(slope, 384 - j, 1))[:, :256]
                act = act + taps_ref[rows, j : j + 1] * moved
                both = moved * own
                both = both[:, :128] + both[:, 128:]
                partial[b][j] = both if s == 0 else partial[b][j] + both
            dy_ref[rows, s * 256 : (s + 1) * 256] = act.astype(BF)
    for b in range(2):
        for j in range(7):
            column = jnp.sum(partial[b][j], axis=1, keepdims=True)
            sums = jnp.where(lanes == b * 8 + j, column, sums)
    sums_ref[...] = sums.T[0:16]


def middle_terms(meta, kv, first, second, grad, taps):
    return pl.pallas_call(
        middle_kernel,
        out_shape=[
            jax.ShapeDtypeStruct((256, 512), BF),
            jax.ShapeDtypeStruct((128, 768), BF),
            jax.ShapeDtypeStruct((16, 128), F32),
        ],
        in_specs=[pl.BlockSpec(memory_space=pltpu.SMEM)] + [pl.BlockSpec(memory_space=pltpu.VMEM)] * 5,
        out_specs=[pl.BlockSpec(memory_space=pltpu.VMEM)] * 3,
    )(meta, kv, first, second, grad, taps)


def product_rows(prod, rows):
    return jnp.concatenate(
        [
            prod[rows, s * 384 + 128 * b : s * 384 + 128 * b + 256]
            for s in range(2)
            for b in range(2)
        ]
    )


def correlation_kernel(prod, up_ref, sums_ref, small_ref):
    small_ref[0:16] = sums_ref[...]
    for g in range(8):
        rows = slice(16 * g, 16 * g + 16)
        above = jnp.concatenate(
            [up_ref[rows, part * 128 : part * 128 + 128] for part in range(4)]
        )
        folded = lax.dot_general(
            above, product_rows(prod, rows), (((0,), (0,)), ((), ())), preferred_element_type=F32
        )
        count = 64
        while count >= 1:
            folded = folded[:count] + pltpu.roll(folded[count : 2 * count], 256 - count, 1)
            count //= 2
        small_ref[16 + g : 17 + g] = folded[:, :128]
        small_ref[24 + g : 25 + g] = folded[:, 128:]


def correlation_terms(prod, up, sums):
    return pl.pallas_call(
        correlation_kernel,
        out_shape=jax.ShapeDtypeStruct((32, 128), F32),
        in_specs=[pl.BlockSpec(memory_space=pltpu.VMEM)] * 3,
        out_specs=pl.BlockSpec(memory_space=pltpu.VMEM),
    )(prod, up, sums)


def response_kernel(meta_ref, prod, band_ref, mixed_ref, resp):
    for g in range(8):
        rows = slice(16 * g, 16 * g + 16)
        total = jnp.dot(product_rows(prod, rows), band_ref[g], preferred_element_type=F32)
        for part in range(4):
            resp[rows, part * 128 : part * 128 + 128] = total[part * 16 : part * 16 + 16]
    for s in range(2):
        place = lax.broadcasted_iota(jnp.int32, (256, 128), 0) + meta_ref[0]
        turned = resp[:, s * 256 : (s + 1) * 256].T
        mixed_ref[s] = jnp.where(place < meta_ref[1 + s], turned, 0.0).astype(BF)


def response_terms(meta, prod, bands):
    return pl.pallas_call(
        response_kernel,
        out_shape=jax.ShapeDtypeStruct((2, 256, 128), BF),
        in_specs=[pl.BlockSpec(memory_space=pltpu.SMEM)] + [pl.BlockSpec(memory_space=pltpu.VMEM)] * 2,
        out_specs=pl.BlockSpec(memory_space=pltpu.VMEM),
        scratch_shapes=[pltpu.VMEM((128, 512), F32)],
    )(meta, prod, bands)


def body(inputs, key_panel, value_panel, short_filters, medium_filters, lengths, cotangent):
    seqs, count, local_width = inputs.shape
    channels = key_panel.shape[1]
    dp = lax.axis_index("dp")
    idx = jnp.stack([dp // 4, dp % 4]).astype(jnp.int32)
    meta = jnp.concatenate(
        [(dp * count).reshape(1).astype(jnp.int32), lengths, (dp % 2).reshape(1).astype(jnp.int32)]
    )

    features = lax.all_gather(inputs.reshape(seqs * count, local_width), "shard", axis=0)
    features = in_hbm(features)
    panels = gather_panels(jnp.concatenate([key_panel, value_panel], axis=1))
    after = shifted(cotangent[:, :144], -1)
    up, product_grad, bands = cotangent_terms(meta, cotangent, after, medium_filters)

    taps = jnp.pad(short_filters.reshape(256, 7), ((0, 0), (0, 1)))
    kv, edges = forward_matmul(idx, features, taps, panels)
    first = dp_pairs(edges, 0)
    second = dp_pairs(edges, 1)
    outgoing, product, sums = middle_terms(meta, in_hbm(kv), first, second, product_grad, taps)
    outgoing = in_hbm(outgoing)
    small = correlation_terms(product, up, sums)
    mixed = response_terms(meta, product, bands)
    key_grad, value_grad, small = reduce_grads(idx, features, outgoing, small)
    short_grad = small[:16].reshape(2, 8, channels)[:, :7].transpose(0, 2, 1)
    medium_grad = jnp.concatenate([small[24:, :1], small[16:24, :0:-1]], axis=1)
    return (mixed, key_grad, value_grad, short_grad, medium_grad)


def solution(mesh):
    return jax.shard_map(
        body,
        mesh=mesh,
        in_specs=(
            P(None, "dp", "shard"),
            P("dp", "shard"),
            P("dp", "shard"),
            P(None, "shard", None),
            P("shard", None),
            P(),
            P(None, "dp", "shard"),
        ),
        out_specs=(
            P(None, "dp", "shard"),
            P("dp", "shard"),
            P("dp", "shard"),
            P(None, "shard", None),
            P("shard", None),
        ),
        check_vma=False,
    )
```
